32 devices in a mesh: dp: 8 (over y, x, core), chan: 4 (over z).
Axes of the slice: x: 2, y: 2, z: 4, core: 2. Of those that a mesh axis runs over, the one named last changes fastest.
Arguments:
- activations: bfloat16 [64, 32, 32, 512], P('dp'), may hold values from -12 to 12
- out_grads: bfloat16 [64, 32, 32, 512], P('dp', None, None, 'chan'), may hold values from -4 to 4
- weight: float32 [512, 3, 3, 512], P('dp', None, None, 'chan'), may hold values from -6 to 6
- momentum: float32 [512, 3, 3, 512], P('dp', None, None, 'chan'), may hold values from -6 to 6
Outputs:
- new_weight: float32 [512, 3, 3, 512], P('dp', None, None, 'chan')
- new_momentum: float32 [512, 3, 3, 512], P('dp', None, None, 'chan')
The draws below stay inside these ranges and needn't reach their ends.
All inputs are finite; a program needn't handle non-finite values.
Results may differ from the reference program's by a relative error of at most 0.0003.
Values sent between devices are 32-bit elements; how exact they have to be, the bound alone decides.
No kernel may reach another device: no remote copies, remote signals or barrier semaphores. Data moves between devices by JAX's collectives and lax.ppermute only.
A program may use at most 64 MiB of HBM per device.

```python
import jax
import jax.numpy as jnp
from jax import lax

CIN = 512
COUT = 512
BATCH = 8
HEIGHT = 32
BREADTH = 32
REPLICAS = 8
N_CHAN = 4


def replica_scales(key_part):
    ramp = jnp.linspace(0.6, 1.8, REPLICAS)
    jitter = jnp.exp(jax.random.uniform(key_part, (REPLICAS,), minval=-0.22, maxval=0.22))
    return (ramp * jitter).reshape(REPLICAS, 1, 1, 1, 1)


def block_shares(key_part, blocks, width):
    ladder = jnp.linspace(0.35, 0.98, blocks).astype(jnp.float32)
    order = jax.random.permutation(key_part, blocks)
    return jnp.repeat(ladder[order], width // blocks)


def draw_activations(key, part):
    common = jax.random.normal(jax.random.fold_in(key, 11), (1, BATCH, HEIGHT, BREADTH, CIN))
    own = jax.random.normal(jax.random.fold_in(key, 12), (REPLICAS, BATCH, HEIGHT, BREADTH, CIN))
    shares = block_shares(jax.random.fold_in(key, 14), REPLICAS, CIN).reshape(1, 1, 1, 1, CIN)
    values = (shares * common + jnp.sqrt(1.0 - shares * shares) * own) * replica_scales(jax.random.fold_in(key, 13))
    values = jnp.clip(values, -12.0, 12.0)
    return values.reshape(REPLICAS * BATCH, HEIGHT, BREADTH, CIN).astype(jnp.bfloat16)


def draw_out_grads(key, part):
    common = jax.random.normal(jax.random.fold_in(key, 21), (1, BATCH, HEIGHT, BREADTH, COUT))
    own = jax.random.normal(jax.random.fold_in(key, 22), (REPLICAS, BATCH, HEIGHT, BREADTH, COUT))
    shares = block_shares(jax.random.fold_in(key, 25), N_CHAN, COUT).reshape(1, 1, 1, 1, COUT)
    channel_ramp = jnp.linspace(0.5, 1.5, COUT).reshape(1, 1, 1, 1, COUT)
    values = (shares * common + jnp.sqrt(1.0 - shares * shares) * own) * replica_scales(jax.random.fold_in(key, 23)) * channel_ramp
    values = values * (0.25 * (BATCH * HEIGHT * BREADTH) ** (-0.5)) * 16.0
    values = jnp.clip(values, -4.0, 4.0)
    return values.reshape(REPLICAS * BATCH, HEIGHT, BREADTH, COUT).astype(jnp.bfloat16)


def block_levels(stream_key, shape, pieces, least, largest):
    gain = 1.0
    for position, shards_of in pieces:
        draws = jax.random.uniform(jax.random.fold_in(jax.random.fold_in(stream_key, 6), position), (shards_of,), jnp.float32, least / len(pieces), largest / len(pieces))
        gain = gain * jnp.repeat(jnp.exp(draws), shape[position] // shards_of).reshape((-1,) + (1,) * (len(shape) - 1 - position))
    return gain


def noise(rng, extent, spread, limit, pieces=(), dtype=jnp.bfloat16):
    drawn = jax.random.normal(rng, extent, jnp.float32) * spread
    if len(pieces) > 0:
        drawn = block_levels(rng, extent, pieces, -0.22, 0.18) * drawn
    return jnp.clip(drawn, min=-limit, max=limit).astype(dtype)


def setup_inputs(seed: int = 0) -> dict:
    splits = jax.random.split(jax.random.key(seed), 5)
    activations = draw_activations(jax.random.fold_in(splits[4], 71), 0)
    out_grads = draw_out_grads(jax.random.fold_in(splits[4], 71), 0)
    weight = noise(splits[2], (CIN, 3, 3, COUT), 1.0, 6.0, ((0, 8), (3, 4)), jnp.float32)
    momentum = noise(splits[3], (CIN, 3, 3, COUT), 1.0, 6.0, ((0, 8), (3, 4)), jnp.float32)
    return {"activations": activations, "out_grads": out_grads, "weight": weight, "momentum": momentum}


def weight_gradient(pair):
    inputs, upstream = pair
    padded = jnp.pad(inputs, ((0, 0), (1, 1), (1, 1), (0, 0)))
    outputs = []
    for row_off in range(3):
        for col_off in range(3):
            window = padded[:, row_off:row_off + HEIGHT, col_off:col_off + BREADTH, :]
            outputs.append(jnp.einsum("bhwc,bhwo->co", window.astype(jnp.float32), upstream.astype(jnp.float32)))
    stacked = jnp.stack(outputs, axis=1)
    return stacked.reshape(CIN, 3, 3, COUT)


def combine(lower_vec, upper_vec):
    crossed = jnp.sum(lower_vec * upper_vec)
    lower_sq = jnp.sum(lower_vec * lower_vec) + 1e-6
    upper_sq = jnp.sum(upper_vec * upper_vec) + 1e-6
    return (1.0 - crossed / (2.0 * lower_sq)) * lower_vec + (1.0 - crossed / (2.0 * upper_sq)) * upper_vec


def reference(activations, out_grads, weight, momentum):
    inputs = activations.reshape(REPLICAS, BATCH, HEIGHT, BREADTH, CIN)
    upstream = out_grads.reshape(REPLICAS, BATCH, HEIGHT, BREADTH, COUT)
    gradients = lax.map(weight_gradient, (inputs, upstream))
    while gradients.shape[0] > 1:
        gradients = jax.vmap(combine)(gradients[0::2], gradients[1::2])
    adasum = gradients[0]
    new_momentum = 0.9 * momentum + adasum
    new_weight = weight - 0.1 * new_momentum
    return new_weight, new_momentum
```

```python
import functools

import jax
import jax.numpy as jnp
from jax import lax
from jax.experimental import pallas as pl
from jax.experimental.pallas import tpu as pltpu
from jax.sharding import PartitionSpec as P


f32, bf16 = jnp.float32, jnp.bfloat16
SM = pl.BlockSpec(memory_space=pltpu.SMEM)
VM = pl.BlockSpec(memory_space=pltpu.VMEM)
HB = pl.BlockSpec(memory_space=pltpu.HBM)
STEPS = 8


def emit(acc, turned, outs, sem, me, cols):
    rows = turned.shape[1] // len(outs)
    for j in range(3):
        turned[j] = acc[j * cols : (j + 1) * cols, :].T
    copies = []
    for k, out in enumerate(outs):
        first = pl.multiple_of(jnp.bitwise_xor(me, k) * rows, rows)
        copies.append(pltpu.make_async_copy(turned.at[:, pl.ds(first, rows), :], out, sem.at[k]))
    for copy in copies:
        copy.start()
    for copy in copies:
        copy.wait()


def first_kernel(parts, me_ref, g_hbm, a_hbm, *rest):
    outs = rest[:parts]
    av, gt, gv, acc, turned, asem, gsem, osem = rest[parts:]
    height, batch, width, cin = av.shape
    cols = gv.shape[3]
    flat = batch * width
    step = height // STEPS
    acopy = [pltpu.make_async_copy(a_hbm.at[:, h], av.at[h], asem.at[h]) for h in range(height)]
    gcopy = [pltpu.make_async_copy(g_hbm.at[:, i * step : (i + 1) * step], gv.at[:, i * step : (i + 1) * step], gsem.at[i]) for i in range(STEPS)]
    for i in range(STEPS):
        gcopy[i].start()
        for h in range(i * step, (i + 1) * step):
            acopy[h].start()
    gt[:, 0:flat] = jnp.zeros((3 * cols, flat), bf16)
    gt[:, (height + 1) * flat : (height + 2) * flat] = jnp.zeros((3 * cols, flat), bf16)
    column = lax.broadcasted_iota(jnp.int32, (cols, flat), 1) % width
    is_last, is_first = column == width - 1, column == 0

    def prepare(i):
        gcopy[i].wait()
        for h in range(i * step, (i + 1) * step):
            g = gv[:, h].reshape(flat, cols).astype(f32).T
            here = slice((h + 1) * flat, (h + 2) * flat)
            gt[0:cols, here] = jnp.where(is_last, 0.0, pltpu.roll(g, flat - 1, 1)).astype(bf16)
            gt[cols : 2 * cols, here] = g.astype(bf16)
            gt[2 * cols : 3 * cols, here] = jnp.where(is_first, 0.0, pltpu.roll(g, 1, 1)).astype(bf16)

    prepare(0)
    for i in range(STEPS):
        for h in range(i * step, (i + 1) * step):
            acopy[h].wait()
        if i + 1 < STEPS:
            prepare(i + 1)
        rhs = av[i * step : (i + 1) * step].reshape(step * flat, cin)
        term = jnp.dot(gt[:, (i * step + 1) * flat : ((i + 1) * step + 1) * flat], rhs, preferred_element_type=f32)
        acc[...] = term if i == 0 else acc[...] + term
    emit(acc, turned, outs, osem, me_ref[0], cols)


def next_kernel(shift, parts, me_ref, gt, av, *rest):
    outs = rest[:parts]
    acc, turned, osem = rest[parts:]
    height, batch, width, cin = av.shape
    flat = batch * width
    cols = gt.shape[0] // 3
    lhs = gt[:, (1 + shift) * flat : (1 + shift + height) * flat]
    acc[...] = jnp.dot(lhs, av[...].reshape(height * flat, cin), preferred_element_type=f32)
    emit(acc, turned, outs, osem, me_ref[0], cols)


def conv_first(a, g, me, parts):
    batch, height, width, cin = a.shape
    cols = g.shape[3]
    flat = batch * width
    res = pl.pallas_call(
        functools.partial(first_kernel, parts),
        out_shape=[jax.ShapeDtypeStruct((3, cin // parts, cols), f32)] * parts
        + [pltpu.VMEM((height, batch, width, cin), bf16), pltpu.VMEM((3 * cols, (height + 2) * flat), bf16)],
        in_specs=[SM, HB, HB],
        out_specs=[HB] * parts + [VM, VM],
        scratch_shapes=[
            pltpu.VMEM((batch, height, width, cols), bf16),
            pltpu.VMEM((3 * cols, cin), f32),
            pltpu.VMEM((3, cin, cols), f32),
            pltpu.SemaphoreType.DMA((height,)),
            pltpu.SemaphoreType.DMA((STEPS,)),
            pltpu.SemaphoreType.DMA((parts,)),
        ],
        compiler_params=pltpu.CompilerParams(vmem_limit_bytes=FIRST_VMEM),
        cost_estimate=pl.CostEstimate(flops=6 * cols * cin * height * flat, bytes_accessed=2 * (a.size + g.size), transcendentals=0),
        name="conv_first",
    )(me, g, a)
    return list(res[:parts]), res[parts], res[parts + 1]


def conv_next(av, gt, me, shift, parts):
    height, batch, width, cin = av.shape
    cols = gt.shape[0] // 3
    return list(pl.pallas_call(
        functools.partial(next_kernel, shift, parts),
        out_shape=[jax.ShapeDtypeStruct((3, cin // parts, cols), f32)] * parts,
        in_specs=[SM, VM, VM],
        out_specs=[HB] * parts,
        scratch_shapes=[pltpu.VMEM((3 * cols, cin), f32), pltpu.VMEM((3, cin, cols), f32), pltpu.SemaphoreType.DMA((parts,))],
        compiler_params=pltpu.CompilerParams(vmem_limit_bytes=NEXT_VMEM),
        cost_estimate=pl.CostEstimate(flops=6 * cols * cin * height * batch * width, bytes_accessed=12 * cin * cols, transcendentals=0),
        name="conv_next",
    )(me, gt, av))


def gram_kernel(chunks, parts, devices, me_ref, *rest):
    blocks = rest[: chunks * parts]
    before = rest[chunks * parts : -1]
    out = rest[-1]
    rows = out.shape[-2]
    me = me_ref[0]
    place = lax.broadcasted_iota(jnp.int32, (rows, 128), 0) * 128 + lax.broadcasted_iota(jnp.int32, (rows, 128), 1)
    total = jnp.zeros((rows, 128), f32)
    for part in before:
        total = total + part[...]
    taps, depth, cols = blocks[0].shape
    group = 4
    for k0 in range(0, parts, group):
        ks = range(k0, min(k0 + group, parts))
        for l0 in range(k0, parts, group):
            pairs = [(k, l) for k in ks for l in range(l0, min(l0 + group, parts)) if k <= l]
            names = sorted({k for k, _ in pairs} | {l for _, l in pairs})
            sums = [jnp.zeros((8, cols), f32) for _ in pairs]
            for c in range(chunks):
                def body(i, sums):
                    tap, r = i // (depth // 8), i % (depth // 8)
                    x = {k: blocks[c * parts + k][tap, pl.ds(pl.multiple_of(r * 8, 8), 8), :] for k in names}
                    return [s + x[k] * x[l] for s, (k, l) in zip(sums, pairs)]
                sums = lax.fori_loop(0, taps * depth // 8, body, sums, unroll=4)
            for s, (k, l) in zip(sums, pairs):
                a, b = jnp.bitwise_xor(me, k), jnp.bitwise_xor(me, l)
                at = jnp.minimum(a, b) * parts + jnp.maximum(a, b)
                total = total + jnp.where(place == at, jnp.sum(s), 0.0)
    if devices:
        for n in range(devices):
            out[n] = total
    else:
        out[...] = total


def gram(chunks, before, me, devices):
    parts = len(chunks[0])
    rows = -(-parts * parts // 128)
    shape = (devices, rows, 128) if devices else (rows, 128)
    flat = [b for chunk in chunks for b in chunk]
    return pl.pallas_call(
        functools.partial(gram_kernel, len(chunks), parts, devices),
        out_shape=jax.ShapeDtypeStruct(shape, f32),
        in_specs=[SM] + [VM] * (len(flat) + len(before)),
        out_specs=VM,
        compiler_params=pltpu.CompilerParams(vmem_limit_bytes=NEXT_VMEM),
        cost_estimate=pl.CostEstimate(flops=flat[0].size * len(chunks) * parts * parts, bytes_accessed=4 * flat[0].size * len(flat), transcendentals=0),
        name="gram",
    )(me, *flat, *before)


def mixes_of(sums, parts):
    rows = sums.shape[0]
    place = lax.broadcasted_iota(jnp.int32, (rows, 128), 0) * 128 + lax.broadcasted_iota(jnp.int32, (rows, 128), 1)
    g = {}
    for a in range(parts):
        for b in range(a, parts):
            g[a, b] = g[b, a] = jnp.sum(jnp.where(place == a * parts + b, sums, 0.0), axis=(0, 1), keepdims=True)
    factors = [None] * parts
    count, width = parts, 1
    while count > 1:
        coef = []
        for k in range(count // 2):
            p, qa, qb = g[2 * k, 2 * k + 1], g[2 * k, 2 * k] + 1e-6, g[2 * k + 1, 2 * k + 1] + 1e-6
            coef += [1.0 - p / (2.0 * qa), 1.0 - p / (2.0 * qb)]
        for r in range(parts):
            c = coef[r // width]
            factors[r] = c if factors[r] is None else factors[r] * c
        count, width = count // 2, width * 2
        new = {}
        for k in range(count):
            for l in range(k, count):
                new[k, l] = new[l, k] = sum(coef[x] * coef[y] * g[x, y] for x in (2 * k, 2 * k + 1) for y in (2 * l, 2 * l + 1))
        g = new
    return factors


def final_kernel(parts, me_ref, sums, weight, momentum, *rest):
    blocks, (new_weight, new_momentum) = rest[:-2], rest[-2:]
    me = me_ref[0]
    total = jnp.sum(sums[...], axis=0)
    factors = mixes_of(total, parts)
    mine = []
    for k in range(parts):
        at = jnp.bitwise_xor(me, k)
        pick = factors[0]
        for r in range(1, parts):
            pick = jnp.where(at == r, factors[r], pick)
        mine.append(pick)
    for i in range(weight.shape[0]):
        for j in range(weight.shape[1]):
            value = 0.9 * momentum[i, j]
            for k in range(parts):
                value = value + mine[k] * blocks[i * parts + k][j]
            new_momentum[i, j] = value
            new_weight[i, j] = weight[i, j] - 0.1 * value


def shards(activations, out_grads, weight, momentum):
    parts = lax.axis_size("dp")
    devices = parts * lax.axis_size("chan")
    me = lax.axis_index("dp").reshape(1).astype(jnp.int32)

    def exchange(blocks):
        return [blocks[0]] + [
            lax.ppermute(blocks[k], "dp", [(r, r ^ k) for r in range(parts)]) for k in range(1, parts)
        ]

    middle, av, gt = conv_first(activations, out_grads, me, parts)
    middle = exchange(middle)
    lower = exchange(conv_next(av, gt, me, 1, parts))
    upper = exchange(conv_next(av, gt, me, -1, parts))
    partial = gram([middle], [], me, 0)
    partial = gram([lower], [partial], me, 0)
    sums = gram([upper], [partial], me, devices)
    sums = lax.all_to_all(sums, ("dp", "chan"), split_axis=0, concat_axis=0, tiled=True)
    w, m = jnp.transpose(weight, (1, 2, 0, 3)), jnp.transpose(momentum, (1, 2, 0, 3))
    new_w, new_m = pl.pallas_call(
        functools.partial(final_kernel, parts),
        out_shape=[jax.ShapeDtypeStruct(w.shape, f32)] * 2,
        in_specs=[SM] + [VM] * (3 + 3 * parts),
        out_specs=[VM, VM],
        compiler_params=pltpu.CompilerParams(vmem_limit_bytes=NEXT_VMEM),
        cost_estimate=pl.CostEstimate(flops=2 * w.size * parts, bytes_accessed=4 * w.size * (parts + 4), transcendentals=0),
        name="final",
    )(me, sums, w, m, *lower, *middle, *upper)
    return jnp.transpose(new_w, (2, 0, 1, 3)), jnp.transpose(new_m, (2, 0, 1, 3))


FIRST_VMEM, NEXT_VMEM = 30 << 20, 30 << 20


def solution(mesh):
    in_specs = (
        P("dp", None, None, None),
        P("dp", None, None, "chan"),
        P("dp", None, None, "chan"),
        P("dp", None, None, "chan"),
    )
    out_specs = (P("dp", None, None, "chan"), P("dp", None, None, "chan"))
    return jax.shard_map(shards, mesh=mesh, in_specs=in_specs, out_specs=out_specs, check_vma=False)
```

```python
import functools

import jax
import jax.numpy as jnp
from jax import lax
from jax.experimental import pallas as pl
from jax.experimental.pallas import tpu as pltpu
from jax.sharding import PartitionSpec as P


f32, bf16 = jnp.float32, jnp.bfloat16
SM = pl.BlockSpec(memory_space=pltpu.SMEM)
VM = pl.BlockSpec(memory_space=pltpu.VMEM)
HB = pl.BlockSpec(memory_space=pltpu.HBM)
STEPS = 8


def emit(acc, turned, outs, sem, me, cols):
    rows = turned.shape[1] // len(outs)
    for j in range(3):
        turned[j] = acc[j * cols : (j + 1) * cols, :].T
    copies = []
    for k, out in enumerate(outs):
        first = pl.multiple_of(jnp.bitwise_xor(me, k) * rows, rows)
        copies.append(pltpu.make_async_copy(turned.at[:, pl.ds(first, rows), :], out, sem.at[k]))
    for copy in copies:
        copy.start()
    for copy in copies:
        copy.wait()


def first_kernel(parts, me_ref, g_hbm, a_hbm, *rest):
    outs = rest[:parts]
    av, gt, gv, acc, turned, asem, gsem, osem = rest[parts:]
    height, batch, width, cin = av.shape
    cols = gv.shape[3]
    flat = batch * width
    step = height // STEPS
    acopy = [pltpu.make_async_copy(a_hbm.at[:, h], av.at[h], asem.at[h]) for h in range(height)]
    gcopy = [pltpu.make_async_copy(g_hbm.at[:, i * step : (i + 1) * step], gv.at[:, i * step : (i + 1) * step], gsem.at[i]) for i in range(STEPS)]
    for i in range(STEPS):
        gcopy[i].start()
        for h in range(i * step, (i + 1) * step):
            acopy[h].start()
    gt[:, 0:flat] = jnp.zeros((3 * cols, flat), bf16)
    gt[:, (height + 1) * flat : (height + 2) * flat] = jnp.zeros((3 * cols, flat), bf16)
    column = lax.broadcasted_iota(jnp.int32, (cols, flat), 1) % width
    is_last, is_first = column == width - 1, column == 0

    def prepare(i):
        gcopy[i].wait()
        for h in range(i * step, (i + 1) * step):
            g = gv[:, h].reshape(flat, cols).astype(f32).T
            here = slice((h + 1) * flat, (h + 2) * flat)
            gt[0:cols, here] = jnp.where(is_last, 0.0, pltpu.roll(g, flat - 1, 1)).astype(bf16)
            gt[cols : 2 * cols, here] = g.astype(bf16)
            gt[2 * cols : 3 * cols, here] = jnp.where(is_first, 0.0, pltpu.roll(g, 1, 1)).astype(bf16)

    prepare(0)
    for i in range(STEPS):
        for h in range(i * step, (i + 1) * step):
            acopy[h].wait()
        if i + 1 < STEPS:
            prepare(i + 1)
        rhs = av[i * step : (i + 1) * step].reshape(step * flat, cin)
        term = jnp.dot(gt[:, (i * step + 1) * flat : ((i + 1) * step + 1) * flat], rhs, preferred_element_type=f32)
        acc[...] = term if i == 0 else acc[...] + term
    emit(acc, turned, outs, osem, me_ref[0], cols)


def next_kernel(shift, parts, me_ref, gt, av, *rest):
    outs = rest[:parts]
    acc, turned, osem = rest[parts:]
    height, batch, width, cin = av.shape
    flat = batch * width
    cols = gt.shape[0] // 3
    lhs = gt[:, (1 + shift) * flat : (1 + shift + height) * flat]
    acc[...] = jnp.dot(lhs, av[...].reshape(height * flat, cin), preferred_element_type=f32)
    emit(acc, turned, outs, osem, me_ref[0], cols)


def conv_first(a, g, me, parts):
    batch, height, width, cin = a.shape
    cols = g.shape[3]
    flat = batch * width
    res = pl.pallas_call(
        functools.partial(first_kernel, parts),
        out_shape=[jax.ShapeDtypeStruct((3, cin // parts, cols), f32)] * parts
        + [pltpu.VMEM((height, batch, width, cin), bf16), pltpu.VMEM((3 * cols, (height + 2) * flat), bf16)],
        in_specs=[SM, HB, HB],
        out_specs=[HB] * parts + [VM, VM],
        scratch_shapes=[
            pltpu.VMEM((batch, height, width, cols), bf16),
            pltpu.VMEM((3 * cols, cin), f32),
            pltpu.VMEM((3, cin, cols), f32),
            pltpu.SemaphoreType.DMA((height,)),
            pltpu.SemaphoreType.DMA((STEPS,)),
            pltpu.SemaphoreType.DMA((parts,)),
        ],
        compiler_params=pltpu.CompilerParams(vmem_limit_bytes=FIRST_VMEM),
        cost_estimate=pl.CostEstimate(flops=6 * cols * cin * height * flat, bytes_accessed=2 * (a.size + g.size), transcendentals=0),
        name="conv_first",
    )(me, g, a)
    return list(res[:parts]), res[parts], res[parts + 1]


def conv_next(av, gt, me, shift, parts):
    height, batch, width, cin = av.shape
    cols = gt.shape[0] // 3
    return list(pl.pallas_call(
        functools.partial(next_kernel, shift, parts),
        out_shape=[jax.ShapeDtypeStruct((3, cin // parts, cols), f32)] * parts,
        in_specs=[SM, VM, VM],
        out_specs=[HB] * parts,
        scratch_shapes=[pltpu.VMEM((3 * cols, cin), f32), pltpu.VMEM((3, cin, cols), f32), pltpu.SemaphoreType.DMA((parts,))],
        compiler_params=pltpu.CompilerParams(vmem_limit_bytes=NEXT_VMEM),
        cost_estimate=pl.CostEstimate(flops=6 * cols * cin * height * batch * width, bytes_accessed=12 * cin * cols, transcendentals=0),
        name="conv_next",
    )(me, gt, av))


def tile_dot(acc, gt, av, tiles, lo, hi, keep):
    _, batch, width, lanes = av.shape[1:]
    flat = batch * width
    rows = gt.shape[0]
    rhs = jnp.concatenate([av[q, lo:hi].reshape((hi - lo) * flat, lanes) for q in tiles], axis=1)
    for i in range(3):
        lhs = gt[:, (lo + 2 - i) * flat : (hi + 2 - i) * flat]
        term = jnp.dot(lhs, rhs, preferred_element_type=f32)
        here = slice(i * rows, (i + 1) * rows)
        acc[here, :] = acc[here, :] + term if keep else term


def tile_emit(acc, turned, outs, sem, me, cols):
    depth = turned.shape[1] // len(outs)
    for j in range(9):
        turned[j] = acc[j * cols : (j + 1) * cols, :].T
    copies = []
    for k, out in enumerate(outs):
        core = jnp.bitwise_xor(jnp.bitwise_and(me, 1), k % 2)
        first = pl.multiple_of((k // 2) * 2 * depth + core * depth, depth)
        copies.append(pltpu.make_async_copy(turned.at[:, pl.ds(first, depth), :], out, sem.at[k]))
    for copy in copies:
        copy.start()
    for copy in copies:
        copy.wait()


def near_kernel(bounds, me_ref, g_hbm, a_hbm, *rest):
    outs = rest[:4]
    av, gt, gv, acc, turned, asem, bsem, gsem, osem = rest[4:]
    _, height, batch, width, lanes = av.shape
    cols = gv.shape[3]
    flat = batch * width
    me = me_ref[0]
    chip = me // 2

    def fetch(q, h, sem):
        first = pl.multiple_of(jnp.bitwise_xor(chip, q) * lanes, lanes)
        return pltpu.make_async_copy(a_hbm.at[:, h, :, pl.ds(first, lanes)], av.at[q, h], sem)

    gcopy = pltpu.make_async_copy(g_hbm, gv, gsem.at[0])
    near = [[fetch(q, h, asem.at[q - 1, h]) for q in (1, 2)] for h in range(height)]
    far = [[fetch(q, h, bsem.at[q // 3, h]) for q in (3, 0)] for h in range(height)]
    gcopy.start()
    for pair in near + far:
        for copy in pair:
            copy.start()
    gt[:, 0:flat] = jnp.zeros((3 * cols, flat), bf16)
    gt[:, (height + 1) * flat : (height + 2) * flat] = jnp.zeros((3 * cols, flat), bf16)
    column = lax.broadcasted_iota(jnp.int32, (cols, flat), 1) % width
    is_last, is_first = column == width - 1, column == 0

    def prepare(lo, hi):
        for h in range(lo, hi):
            g = gv[:, h].reshape(flat, cols).astype(f32).T
            here = slice((h + 1) * flat, (h + 2) * flat)
            gt[0:cols, here] = jnp.where(is_last, 0.0, pltpu.roll(g, flat - 1, 1)).astype(bf16)
            gt[cols : 2 * cols, here] = g.astype(bf16)
            gt[2 * cols : 3 * cols, here] = jnp.where(is_first, 0.0, pltpu.roll(g, 1, 1)).astype(bf16)

    gcopy.wait()
    prepare(0, bounds[1] + 1)
    for i in range(len(bounds) - 1):
        lo, hi = bounds[i], bounds[i + 1]
        for h in range(lo, hi):
            for copy in near[h]:
                copy.wait()
        if i + 2 < len(bounds):
            prepare(hi + 1, min(bounds[i + 2] + 1, height))
        tile_dot(acc, gt, av, (1, 2), lo, hi, i > 0)
    tile_emit(acc, turned, outs, osem, me, cols)
    for pair in far:
        for copy in pair:
            copy.wait()


def far_kernel(me_ref, gt, av, *rest):
    outs = rest[:4]
    acc, turned, osem = rest[4:]
    tile_dot(acc, gt, av, (3, 0), 0, av.shape[1], False)
    tile_emit(acc, turned, outs, osem, me_ref[0], gt.shape[0] // 3)


def near_blocks(a, g, me):
    batch, height, width, cin = a.shape
    cols = g.shape[3]
    lanes, flat = cin // 4, batch * width
    block = jax.ShapeDtypeStruct((9, lanes // 2, cols), f32)
    res = pl.pallas_call(
        functools.partial(near_kernel, [0, height // 8, height // 2, height]),
        out_shape=[block] * 4 + [pltpu.VMEM((4, height, batch, width, lanes), bf16), pltpu.VMEM((3 * cols, (height + 2) * flat), bf16)],
        in_specs=[SM, HB, HB],
        out_specs=[HB] * 4 + [VM, VM],
        scratch_shapes=[
            pltpu.VMEM((batch, height, width, cols), bf16),
            pltpu.VMEM((9 * cols, 2 * lanes), f32),
            pltpu.VMEM((9, 2 * lanes, cols), f32),
            pltpu.SemaphoreType.DMA((2, height)),
            pltpu.SemaphoreType.DMA((2, height)),
            pltpu.SemaphoreType.DMA((1,)),
            pltpu.SemaphoreType.DMA((4,)),
        ],
        compiler_params=pltpu.CompilerParams(vmem_limit_bytes=NEAR_VMEM),
        cost_estimate=pl.CostEstimate(flops=36 * cols * lanes * height * flat, bytes_accessed=2 * (a.size + g.size), transcendentals=0),
        name="conv_near",
    )(me, g, a)
    return list(res[:4]), res[4], res[5]


def far_blocks(av, gt, me):
    _, height, batch, width, lanes = av.shape
    cols = gt.shape[0] // 3
    block = jax.ShapeDtypeStruct((9, lanes // 2, cols), f32)
    return list(pl.pallas_call(
        far_kernel,
        out_shape=[block] * 4,
        in_specs=[SM, VM, VM],
        out_specs=[HB] * 4,
        scratch_shapes=[pltpu.VMEM((9 * cols, 2 * lanes), f32), pltpu.VMEM((9, 2 * lanes, cols), f32), pltpu.SemaphoreType.DMA((4,))],
        compiler_params=pltpu.CompilerParams(vmem_limit_bytes=NEXT_VMEM),
        cost_estimate=pl.CostEstimate(flops=36 * cols * lanes * height * batch * width, bytes_accessed=72 * lanes * cols, transcendentals=0),
        name="conv_far",
    )(me, gt, av))


def gram_kernel(pairs, parts, devices, me_ref, *rest):
    blocks, out, rowsums = rest[:-2], rest[-2], rest[-1]
    chunks = len(blocks) // parts
    before = blocks[chunks * parts :]
    me = me_ref[0]
    taps, depth, cols = blocks[0].shape
    rowsums[...] = jnp.zeros_like(rowsums)
    for first in range(0, len(pairs), 18):
        some = pairs[first : first + 18]
        names = sorted({n for pair in some for n in pair})
        sums = [jnp.zeros((8, cols), f32) for _ in some]
        for c in range(chunks):
            def body(i, sums):
                tap, r = i // (depth // 8), i % (depth // 8)
                x = {k: blocks[c * parts + k][tap, pl.ds(pl.multiple_of(r * 8, 8), 8), :] for k in names}
                return [s + x[k] * x[l] for s, (k, l) in zip(sums, some)]

            sums = lax.fori_loop(0, taps * depth // 8, body, sums, unroll=4)
        for s, (k, l) in zip(sums, some):
            rowsums[k * parts + l : k * parts + l + 1, :] = jnp.sum(s, axis=0, keepdims=True)
    number = lax.broadcasted_iota(jnp.int32, (parts * parts, 128), 0)
    a, b = jnp.bitwise_xor(number // parts, me), jnp.bitwise_xor(number % parts, me)
    at = jnp.minimum(a, b) * parts + jnp.maximum(a, b)
    place = lax.broadcasted_iota(jnp.int32, (parts * parts, 128), 1)
    values = jnp.sum(rowsums[...], axis=1, keepdims=True)
    for r in range(out.shape[-2]):
        total = jnp.sum(jnp.where(at == place + r * 128, values, 0.0), axis=0, keepdims=True)
        for part in before:
            total = total + part[r : r + 1, :]
        for n in range(max(devices, 1)):
            if devices:
                out[n, r : r + 1, :] = total
            else:
                out[r : r + 1, :] = total


def gram(chunks, pairs, before, me, devices):
    parts = len(chunks[0])
    rows = -(-parts * parts // 128)
    shape = (devices, rows, 128) if devices else (rows, 128)
    flat = [b for chunk in chunks for b in chunk]
    return pl.pallas_call(
        functools.partial(gram_kernel, pairs, parts, devices),
        out_shape=jax.ShapeDtypeStruct(shape, f32),
        in_specs=[SM] + [VM] * (len(flat) + len(before)),
        out_specs=VM,
        scratch_shapes=[pltpu.VMEM((parts * parts, flat[0].shape[2]), f32)],
        compiler_params=pltpu.CompilerParams(vmem_limit_bytes=NEXT_VMEM),
        cost_estimate=pl.CostEstimate(flops=2 * flat[0].size * len(chunks) * len(pairs), bytes_accessed=4 * flat[0].size * len(flat), transcendentals=0),
        name="gram",
    )(me, *flat, *before)


def mixes_of(sums, parts):
    rows = sums.shape[0]
    place = lax.broadcasted_iota(jnp.int32, (rows, 128), 0) * 128 + lax.broadcasted_iota(jnp.int32, (rows, 128), 1)
    g = {}
    for a in range(parts):
        for b in range(a, parts):
            g[a, b] = g[b, a] = jnp.sum(jnp.where(place == a * parts + b, sums, 0.0), axis=(0, 1), keepdims=True)
    factors = [None] * parts
    count, width = parts, 1
    while count > 1:
        coef = []
        for k in range(count // 2):
            p, qa, qb = g[2 * k, 2 * k + 1], g[2 * k, 2 * k] + 1e-6, g[2 * k + 1, 2 * k + 1] + 1e-6
            coef += [1.0 - p / (2.0 * qa), 1.0 - p / (2.0 * qb)]
        for r in range(parts):
            c = coef[r // width]
            factors[r] = c if factors[r] is None else factors[r] * c
        count, width = count // 2, width * 2
        new = {}
        for k in range(count):
            for l in range(k, count):
                new[k, l] = new[l, k] = sum(coef[x] * coef[y] * g[x, y] for x in (2 * k, 2 * k + 1) for y in (2 * l, 2 * l + 1))
        g = new
    return factors


def final_kernel(parts, me_ref, sums, weight, momentum, *rest):
    blocks, (new_weight, new_momentum) = rest[:-2], rest[-2:]
    me = me_ref[0]
    total = jnp.sum(sums[...], axis=0)
    factors = mixes_of(total, parts)
    mine = []
    for k in range(parts):
        at = jnp.bitwise_xor(me, k)
        pick = factors[0]
        for r in range(1, parts):
            pick = jnp.where(at == r, factors[r], pick)
        mine.append(pick)
    taps = blocks[0].shape[0]
    for n in range(weight.shape[0]):
        value = 0.9 * momentum[n]
        for k in range(parts):
            value = value + mine[k] * blocks[n // taps * parts + k][n % taps]
        new_momentum[n] = value
        new_weight[n] = weight[n] - 0.1 * value


def finish(sums, weight, momentum, chunks, me):
    parts = len(chunks[0])
    depth, cols = weight.shape[0], weight.shape[3]
    w = jnp.transpose(weight, (1, 2, 0, 3)).reshape(9, depth, cols)
    m = jnp.transpose(momentum, (1, 2, 0, 3)).reshape(9, depth, cols)
    flat = [b for chunk in chunks for b in chunk]
    outs = pl.pallas_call(
        functools.partial(final_kernel, parts),
        out_shape=[jax.ShapeDtypeStruct(w.shape, f32)] * 2,
        in_specs=[SM] + [VM] * (3 + len(flat)),
        out_specs=[VM, VM],
        compiler_params=pltpu.CompilerParams(vmem_limit_bytes=NEXT_VMEM),
        cost_estimate=pl.CostEstimate(flops=2 * w.size * parts, bytes_accessed=4 * w.size * (parts + 4), transcendentals=0),
        name="final",
    )(me, sums, w, m, *flat)
    return tuple(jnp.transpose(x.reshape(3, 3, depth, cols), (2, 0, 1, 3)) for x in outs)


def upper_pairs(parts):
    return [(k, l) for k in range(parts) for l in range(k, parts)]


def send(block, k, parts):
    return lax.ppermute(block, "dp", [(r, r ^ k) for r in range(parts)])


def by_rows(activations, out_grads, me, parts):
    def exchange(blocks):
        return blocks[:1] + [send(blocks[k], k, parts) for k in range(1, parts)]

    middle, av, gt = conv_first(activations, out_grads, me, parts)
    middle = exchange(middle)
    lower = exchange(conv_next(av, gt, me, 1, parts))
    upper = exchange(conv_next(av, gt, me, -1, parts))
    return [lower, middle, upper], upper_pairs(parts), []


def by_chips(activations, out_grads, me, parts):
    near, av, gt = near_blocks(activations, out_grads, me)
    near = [send(near[k - 2], k, parts) for k in range(2, 6)]
    far = far_blocks(av, gt, me)
    far = [send(far[k], 6 + k, parts) for k in range(2)] + [far[2], send(far[3], 1, parts)]
    blocks = far[2:] + near
    early = [pair for pair in upper_pairs(parts) if pair[1] < 6]
    partial = gram([blocks + [blocks[0]] * 2], early, [], me, 0)
    blocks = blocks + far[:2]
    return [blocks], [pair for pair in upper_pairs(parts) if pair[1] >= 6], [partial]


def shards(activations, out_grads, weight, momentum):
    parts = lax.axis_size("dp")
    devices = parts * lax.axis_size("chan")
    me = lax.axis_index("dp").reshape(1).astype(jnp.int32)
    four = parts == 8 and activations.shape[3] % 512 == 0
    chunks, pairs, before = (by_chips if four else by_rows)(activations, out_grads, me, parts)
    sums = gram(chunks, pairs, before, me, devices)
    sums = lax.all_to_all(sums, ("dp", "chan"), split_axis=0, concat_axis=0, tiled=True)
    return finish(sums, weight, momentum, chunks, me)


FIRST_VMEM, NEXT_VMEM, NEAR_VMEM = 30 << 20, 30 << 20, 46 << 20


def solution(mesh):
    in_specs = (
        P("dp", None, None, None),
        P("dp", None, None, "chan"),
        P("dp", None, None, "chan"),
        P("dp", None, None, "chan"),
    )
    out_specs = (P("dp", None, None, "chan"), P("dp", None, None, "chan"))
    return jax.shard_map(shards, mesh=mesh, in_specs=in_specs, out_specs=out_specs, check_vma=False)
```

```python
import functools

import jax
import jax.numpy as jnp
from jax import lax
from jax.experimental import pallas as pl
from jax.experimental.pallas import tpu as pltpu
from jax.sharding import PartitionSpec as P


f32, bf16 = jnp.float32, jnp.bfloat16
SM = pl.BlockSpec(memory_space=pltpu.SMEM)
VM = pl.BlockSpec(memory_space=pltpu.VMEM)
HB = pl.BlockSpec(memory_space=pltpu.HBM)
STEPS = 8


def emit(acc, turned, outs, sem, me, cols):
    rows = turned.shape[1] // len(outs)
    for j in range(3):
        turned[j] = acc[j * cols : (j + 1) * cols, :].T
    copies = []
    for k, out in enumerate(outs):
        first = pl.multiple_of(jnp.bitwise_xor(me, k) * rows, rows)
        copies.append(pltpu.make_async_copy(turned.at[:, pl.ds(first, rows), :], out, sem.at[k]))
    for copy in copies:
        copy.start()
    for copy in copies:
        copy.wait()


def first_kernel(parts, me_ref, g_hbm, a_hbm, *rest):
    outs = rest[:parts]
    av, gt, gv, acc, turned, asem, gsem, osem = rest[parts:]
    height, batch, width, cin = av.shape
    cols = gv.shape[3]
    flat = batch * width
    step = height // STEPS
    acopy = [pltpu.make_async_copy(a_hbm.at[:, h], av.at[h], asem.at[h]) for h in range(height)]
    gcopy = [pltpu.make_async_copy(g_hbm.at[:, i * step : (i + 1) * step], gv.at[:, i * step : (i + 1) * step], gsem.at[i]) for i in range(STEPS)]
    for i in range(STEPS):
        gcopy[i].start()
        for h in range(i * step, (i + 1) * step):
            acopy[h].start()
    gt[:, 0:flat] = jnp.zeros((3 * cols, flat), bf16)
    gt[:, (height + 1) * flat : (height + 2) * flat] = jnp.zeros((3 * cols, flat), bf16)
    column = lax.broadcasted_iota(jnp.int32, (cols, flat), 1) % width
    is_last, is_first = column == width - 1, column == 0

    def prepare(i):
        gcopy[i].wait()
        for h in range(i * step, (i + 1) * step):
            g = gv[:, h].reshape(flat, cols).astype(f32).T
            here = slice((h + 1) * flat, (h + 2) * flat)
            gt[0:cols, here] = jnp.where(is_last, 0.0, pltpu.roll(g, flat - 1, 1)).astype(bf16)
            gt[cols : 2 * cols, here] = g.astype(bf16)
            gt[2 * cols : 3 * cols, here] = jnp.where(is_first, 0.0, pltpu.roll(g, 1, 1)).astype(bf16)

    prepare(0)
    for i in range(STEPS):
        for h in range(i * step, (i + 1) * step):
            acopy[h].wait()
        if i + 1 < STEPS:
            prepare(i + 1)
        rhs = av[i * step : (i + 1) * step].reshape(step * flat, cin)
        term = jnp.dot(gt[:, (i * step + 1) * flat : ((i + 1) * step + 1) * flat], rhs, preferred_element_type=f32)
        acc[...] = term if i == 0 else acc[...] + term
    emit(acc, turned, outs, osem, me_ref[0], cols)


def next_kernel(shift, parts, me_ref, gt, av, *rest):
    outs = rest[:parts]
    acc, turned, osem = rest[parts:]
    height, batch, width, cin = av.shape
    flat = batch * width
    cols = gt.shape[0] // 3
    lhs = gt[:, (1 + shift) * flat : (1 + shift + height) * flat]
    acc[...] = jnp.dot(lhs, av[...].reshape(height * flat, cin), preferred_element_type=f32)
    emit(acc, turned, outs, osem, me_ref[0], cols)


def conv_first(a, g, me, parts):
    batch, height, width, cin = a.shape
    cols = g.shape[3]
    flat = batch * width
    res = pl.pallas_call(
        functools.partial(first_kernel, parts),
        out_shape=[jax.ShapeDtypeStruct((3, cin // parts, cols), f32)] * parts
        + [pltpu.VMEM((height, batch, width, cin), bf16), pltpu.VMEM((3 * cols, (height + 2) * flat), bf16)],
        in_specs=[SM, HB, HB],
        out_specs=[HB] * parts + [VM, VM],
        scratch_shapes=[
            pltpu.VMEM((batch, height, width, cols), bf16),
            pltpu.VMEM((3 * cols, cin), f32),
            pltpu.VMEM((3, cin, cols), f32),
            pltpu.SemaphoreType.DMA((height,)),
            pltpu.SemaphoreType.DMA((STEPS,)),
            pltpu.SemaphoreType.DMA((parts,)),
        ],
        compiler_params=pltpu.CompilerParams(vmem_limit_bytes=FIRST_VMEM),
        cost_estimate=pl.CostEstimate(flops=6 * cols * cin * height * flat, bytes_accessed=2 * (a.size + g.size), transcendentals=0),
        name="conv_first",
    )(me, g, a)
    return list(res[:parts]), res[parts], res[parts + 1]


def conv_next(av, gt, me, shift, parts):
    height, batch, width, cin = av.shape
    cols = gt.shape[0] // 3
    return list(pl.pallas_call(
        functools.partial(next_kernel, shift, parts),
        out_shape=[jax.ShapeDtypeStruct((3, cin // parts, cols), f32)] * parts,
        in_specs=[SM, VM, VM],
        out_specs=[HB] * parts,
        scratch_shapes=[pltpu.VMEM((3 * cols, cin), f32), pltpu.VMEM((3, cin, cols), f32), pltpu.SemaphoreType.DMA((parts,))],
        compiler_params=pltpu.CompilerParams(vmem_limit_bytes=NEXT_VMEM),
        cost_estimate=pl.CostEstimate(flops=6 * cols * cin * height * batch * width, bytes_accessed=12 * cin * cols, transcendentals=0),
        name="conv_next",
    )(me, gt, av))


def tile_terms(gt, rhs, lo, hi, flat, i):
    return jnp.dot(gt[:, (lo + 2 - i) * flat : (hi + 2 - i) * flat], rhs, preferred_element_type=f32)


def tile_columns(av, chip, tiles, lo, hi):
    _, batch, width, cin = av.shape
    lanes = cin // 4
    firsts = [pl.multiple_of(jnp.bitwise_xor(chip, q) * lanes, lanes) for q in tiles]
    return jnp.concatenate([av[lo:hi, :, :, pl.ds(f, lanes)].reshape((hi - lo) * batch * width, lanes) for f in firsts], axis=1)


def tile_store(value, i, outs, me, cols):
    depth = outs[0].shape[1]
    is_lower = jnp.bitwise_and(me, 1) == 0
    for q in range(len(outs) // 2):
        for j in range(3):
            turned = value[j * cols : (j + 1) * cols, q * 2 * depth : (q + 1) * 2 * depth].T
            lower, upper = turned[:depth], turned[depth:]
            outs[2 * q][3 * i + j] = jnp.where(is_lower, lower, upper)
            outs[2 * q + 1][3 * i + j] = jnp.where(is_lower, upper, lower)


def near_kernel(bounds, me_ref, g_hbm, a_hbm, *rest):
    outs = rest[:4]
    av, gt, gv, acc, asem, gsem = rest[4:]
    height, batch, width, _ = av.shape
    cols = gv.shape[3]
    flat = batch * width
    rows = 3 * cols
    me = me_ref[0]
    gends = [0] + [min(b + 1, height) for b in bounds[1:]]
    gcopy = [pltpu.make_async_copy(g_hbm.at[:, h], gv.at[:, h], gsem.at[h]) for h in range(height)]
    acopy = [pltpu.make_async_copy(a_hbm.at[:, h], av.at[h], asem.at[h]) for h in range(height)]
    for copy in gcopy[: gends[1]] + acopy[: bounds[1]] + gcopy[gends[1] :] + acopy[bounds[1] :]:
        copy.start()
    gt[:, 0:flat] = jnp.zeros((rows, flat), bf16)
    gt[:, (height + 1) * flat : (height + 2) * flat] = jnp.zeros((rows, flat), bf16)
    column = lax.broadcasted_iota(jnp.int32, (cols, flat), 1) % width
    is_last, is_first = column == width - 1, column == 0

    def prepare(lo, hi):
        for h in range(lo, hi):
            g = gv[:, h].reshape(flat, cols).astype(f32).T
            here = slice((h + 1) * flat, (h + 2) * flat)
            gt[0:cols, here] = jnp.where(is_last, 0.0, pltpu.roll(g, flat - 1, 1)).astype(bf16)
            gt[cols : 2 * cols, here] = g.astype(bf16)
            gt[2 * cols : 3 * cols, here] = jnp.where(is_first, 0.0, pltpu.roll(g, 1, 1)).astype(bf16)

    for h in range(gends[1]):
        gcopy[h].wait()

    @pl.when(me >= 0)
    def _():
        prepare(0, gends[1])

    for n in range(len(bounds) - 1):
        lo, hi = bounds[n], bounds[n + 1]
        for h in range(lo, hi):
            acopy[h].wait()
        if n + 2 < len(bounds):
            for h in range(gends[n + 1], gends[n + 2]):
                gcopy[h].wait()

        @pl.when(me >= 0)
        def _(n=n, lo=lo, hi=hi):
            is_end = n + 2 == len(bounds)
            if not is_end:
                prepare(gends[n + 1], gends[n + 2])
            rhs = tile_columns(av, me // 2, (1, 2), lo, hi)
            for i in range(3):
                here = slice(i * rows, (i + 1) * rows)
                term = tile_terms(gt, rhs, lo, hi, flat, i)
                if n > 0:
                    term = acc[here, :] + term
                if is_end:
                    tile_store(term, i, outs, me, cols)
                else:
                    acc[here, :] = term


def far_kernel(me_ref, gt, av, *outs):
    height, batch, width, _ = av.shape
    me = me_ref[0]
    rhs = tile_columns(av, me // 2, (3, 0), 0, height)
    for i in range(3):
        tile_store(tile_terms(gt, rhs, 0, height, batch * width, i), i, outs, me, gt.shape[0] // 3)


def near_blocks(a, g, me):
    batch, height, width, cin = a.shape
    cols = g.shape[3]
    lanes, flat = cin // 4, batch * width
    block = jax.ShapeDtypeStruct((9, lanes // 2, cols), f32)
    res = pl.pallas_call(
        functools.partial(near_kernel, [0, height // 8, height * 3 // 8, height * 11 // 16, height]),
        out_shape=[block] * 4 + [pltpu.VMEM((height, batch, width, cin), bf16), pltpu.VMEM((3 * cols, (height + 2) * flat), bf16)],
        in_specs=[SM, HB, HB],
        out_specs=[VM] * 6,
        scratch_shapes=[
            pltpu.VMEM((batch, height, width, cols), bf16),
            pltpu.VMEM((9 * cols, 2 * lanes), f32),
            pltpu.SemaphoreType.DMA((height,)),
            pltpu.SemaphoreType.DMA((height,)),
        ],
        compiler_params=pltpu.CompilerParams(vmem_limit_bytes=NEAR_VMEM),
        cost_estimate=pl.CostEstimate(flops=36 * cols * lanes * height * flat, bytes_accessed=2 * (a.size + g.size), transcendentals=0),
        name="conv_near",
    )(me, g, a)
    return list(res[:4]), res[4], res[5]


def far_blocks(av, gt, me):
    height, batch, width, cin = av.shape
    lanes = cin // 4
    cols = gt.shape[0] // 3
    block = jax.ShapeDtypeStruct((9, lanes // 2, cols), f32)
    return list(pl.pallas_call(
        far_kernel,
        out_shape=[block] * 4,
        in_specs=[SM, VM, VM],
        out_specs=[VM] * 4,
        compiler_params=pltpu.CompilerParams(vmem_limit_bytes=NEXT_VMEM),
        cost_estimate=pl.CostEstimate(flops=36 * cols * lanes * height * batch * width, bytes_accessed=72 * lanes * cols, transcendentals=0),
        name="conv_far",
    )(me, gt, av))


def gram_kernel(pairs, parts, devices, me_ref, *rest):
    blocks, out, rowsums = rest[:-2], rest[-2], rest[-1]
    chunks = len(blocks) // parts
    before = blocks[chunks * parts :]
    me = me_ref[0]
    taps, depth, cols = blocks[0].shape
    rowsums[...] = jnp.zeros_like(rowsums)
    for first in range(0, len(pairs), 18):
        some = pairs[first : first + 18]
        names = sorted({n for pair in some for n in pair})
        sums = [jnp.zeros((8, cols), f32) for _ in some]
        for c in range(chunks):
            def body(i, sums):
                tap, r = i // (depth // 8), i % (depth // 8)
                x = {k: blocks[c * parts + k][tap, pl.ds(pl.multiple_of(r * 8, 8), 8), :] for k in names}
                return [s + x[k] * x[l] for s, (k, l) in zip(sums, some)]

            sums = lax.fori_loop(0, taps * depth // 8, body, sums, unroll=4)
        for s, (k, l) in zip(sums, some):
            rowsums[k * parts + l : k * parts + l + 1, :] = jnp.sum(s, axis=0, keepdims=True)
    number = lax.broadcasted_iota(jnp.int32, (parts * parts, 128), 0)
    a, b = jnp.bitwise_xor(number // parts, me), jnp.bitwise_xor(number % parts, me)
    at = jnp.minimum(a, b) * parts + jnp.maximum(a, b)
    place = lax.broadcasted_iota(jnp.int32, (parts * parts, 128), 1)
    values = jnp.sum(rowsums[...], axis=1, keepdims=True)
    for r in range(out.shape[-2]):
        total = jnp.sum(jnp.where(at == place + r * 128, values, 0.0), axis=0, keepdims=True)
        for part in before:
            total = total + part[r : r + 1, :]
        for n in range(max(devices, 1)):
            if devices:
                out[n, r : r + 1, :] = total
            else:
                out[r : r + 1, :] = total


def gram(chunks, pairs, before, me, devices):
    parts = len(chunks[0])
    rows = -(-parts * parts // 128)
    shape = (devices, rows, 128) if devices else (rows, 128)
    flat = [b for chunk in chunks for b in chunk]
    return pl.pallas_call(
        functools.partial(gram_kernel, pairs, parts, devices),
        out_shape=jax.ShapeDtypeStruct(shape, f32),
        in_specs=[SM] + [VM] * (len(flat) + len(before)),
        out_specs=VM,
        scratch_shapes=[pltpu.VMEM((parts * parts, flat[0].shape[2]), f32)],
        compiler_params=pltpu.CompilerParams(vmem_limit_bytes=NEXT_VMEM),
        cost_estimate=pl.CostEstimate(flops=2 * flat[0].size * len(chunks) * len(pairs), bytes_accessed=4 * flat[0].size * len(flat), transcendentals=0),
        name="gram",
    )(me, *flat, *before)


def mixes_of(sums, parts):
    rows = sums.shape[0]
    place = lax.broadcasted_iota(jnp.int32, (rows, 128), 0) * 128 + lax.broadcasted_iota(jnp.int32, (rows, 128), 1)
    g = {}
    for a in range(parts):
        for b in range(a, parts):
            g[a, b] = g[b, a] = jnp.sum(jnp.where(place == a * parts + b, sums, 0.0), axis=(0, 1), keepdims=True)
    factors = [None] * parts
    count, width = parts, 1
    while count > 1:
        coef = []
        for k in range(count // 2):
            p, qa, qb = g[2 * k, 2 * k + 1], g[2 * k, 2 * k] + 1e-6, g[2 * k + 1, 2 * k + 1] + 1e-6
            coef += [1.0 - p / (2.0 * qa), 1.0 - p / (2.0 * qb)]
        for r in range(parts):
            c = coef[r // width]
            factors[r] = c if factors[r] is None else factors[r] * c
        count, width = count // 2, width * 2
        new = {}
        for k in range(count):
            for l in range(k, count):
                new[k, l] = new[l, k] = sum(coef[x] * coef[y] * g[x, y] for x in (2 * k, 2 * k + 1) for y in (2 * l, 2 * l + 1))
        g = new
    return factors


def final_kernel(parts, me_ref, sums, weight, momentum, *rest):
    blocks, (new_weight, new_momentum) = rest[:-2], rest[-2:]
    me = me_ref[0]
    total = jnp.sum(sums[...], axis=0)
    factors = mixes_of(total, parts)
    mine = []
    for k in range(parts):
        at = jnp.bitwise_xor(me, k)
        pick = factors[0]
        for r in range(1, parts):
            pick = jnp.where(at == r, factors[r], pick)
        mine.append(pick)
    taps = blocks[0].shape[0]
    for n in range(weight.shape[0]):
        value = 0.9 * momentum[n]
        for k in range(parts):
            value = value + mine[k] * blocks[n // taps * parts + k][n % taps]
        new_momentum[n] = value
        new_weight[n] = weight[n] - 0.1 * value


def finish(sums, weight, momentum, chunks, me):
    parts = len(chunks[0])
    depth, cols = weight.shape[0], weight.shape[3]
    w = jnp.transpose(weight, (1, 2, 0, 3)).reshape(9, depth, cols)
    m = jnp.transpose(momentum, (1, 2, 0, 3)).reshape(9, depth, cols)
    flat = [b for chunk in chunks for b in chunk]
    outs = pl.pallas_call(
        functools.partial(final_kernel, parts),
        out_shape=[jax.ShapeDtypeStruct(w.shape, f32)] * 2,
        in_specs=[SM] + [VM] * (3 + len(flat)),
        out_specs=[VM, VM],
        compiler_params=pltpu.CompilerParams(vmem_limit_bytes=NEXT_VMEM),
        cost_estimate=pl.CostEstimate(flops=2 * w.size * parts, bytes_accessed=4 * w.size * (parts + 4), transcendentals=0),
        name="final",
    )(me, sums, w, m, *flat)
    return tuple(jnp.transpose(x.reshape(3, 3, depth, cols), (2, 0, 1, 3)) for x in outs)


def upper_pairs(parts):
    return [(k, l) for k in range(parts) for l in range(k, parts)]


def send(block, k, parts):
    return lax.ppermute(block, "dp", [(r, r ^ k) for r in range(parts)])


def by_rows(activations, out_grads, me, parts):
    def exchange(blocks):
        return blocks[:1] + [send(blocks[k], k, parts) for k in range(1, parts)]

    middle, av, gt = conv_first(activations, out_grads, me, parts)
    middle = exchange(middle)
    lower = exchange(conv_next(av, gt, me, 1, parts))
    upper = exchange(conv_next(av, gt, me, -1, parts))
    return [lower, middle, upper], upper_pairs(parts), []


def by_chips(activations, out_grads, me, parts):
    near, av, gt = near_blocks(activations, out_grads, me)
    near = [send(near[k - 2], k, parts) for k in range(2, 6)]
    far = far_blocks(av, gt, me)
    far = [send(far[k], 6 + k, parts) for k in range(2)] + [far[2], send(far[3], 1, parts)]
    blocks = far[2:] + near
    early = [pair for pair in upper_pairs(parts) if pair[1] < 6]
    partial = gram([blocks + [blocks[0]] * 2], early, [], me, 0)
    blocks = blocks + far[:2]
    return [blocks], [pair for pair in upper_pairs(parts) if pair[1] >= 6], [partial]


def shards(activations, out_grads, weight, momentum):
    parts = lax.axis_size("dp")
    devices = parts * lax.axis_size("chan")
    me = lax.axis_index("dp").reshape(1).astype(jnp.int32)
    four = parts == 8 and activations.shape[3] % 512 == 0
    chunks, pairs, before = (by_chips if four else by_rows)(activations, out_grads, me, parts)
    sums = gram(chunks, pairs, before, me, devices)
    sums = lax.all_to_all(sums, ("dp", "chan"), split_axis=0, concat_axis=0, tiled=True)
    return finish(sums, weight, momentum, chunks, me)


FIRST_VMEM, NEXT_VMEM, NEAR_VMEM = 30 << 20, 30 << 20, 38 << 20


def solution(mesh):
    in_specs = (
        P("dp", None, None, None),
        P("dp", None, None, "chan"),
        P("dp", None, None, "chan"),
        P("dp", None, None, "chan"),
    )
    out_specs = (P("dp", None, None, "chan"), P("dp", None, None, "chan"))
    return jax.shard_map(shards, mesh=mesh, in_specs=in_specs, out_specs=out_specs, check_vma=False)
```

```python
import functools

import jax
import jax.numpy as jnp
from jax import lax
from jax.experimental import pallas as pl
from jax.experimental.pallas import tpu as pltpu
from jax.sharding import PartitionSpec as P


f32, bf16 = jnp.float32, jnp.bfloat16
SM = pl.BlockSpec(memory_space=pltpu.SMEM)
VM = pl.BlockSpec(memory_space=pltpu.VMEM)
HB = pl.BlockSpec(memory_space=pltpu.HBM)
STEPS = 8


def emit(acc, turned, outs, sem, me, cols):
    rows = turned.shape[1] // len(outs)
    for j in range(3):
        turned[j] = acc[j * cols : (j + 1) * cols, :].T
    copies = []
    for k, out in enumerate(outs):
        first = pl.multiple_of(jnp.bitwise_xor(me, k) * rows, rows)
        copies.append(pltpu.make_async_copy(turned.at[:, pl.ds(first, rows), :], out, sem.at[k]))
    for copy in copies:
        copy.start()
    for copy in copies:
        copy.wait()


def first_kernel(parts, me_ref, g_hbm, a_hbm, *rest):
    outs = rest[:parts]
    av, gt, gv, acc, turned, asem, gsem, osem = rest[parts:]
    height, batch, width, cin = av.shape
    cols = gv.shape[3]
    flat = batch * width
    step = height // STEPS
    acopy = [pltpu.make_async_copy(a_hbm.at[:, h], av.at[h], asem.at[h]) for h in range(height)]
    gcopy = [pltpu.make_async_copy(g_hbm.at[:, i * step : (i + 1) * step], gv.at[:, i * step : (i + 1) * step], gsem.at[i]) for i in range(STEPS)]
    for i in range(STEPS):
        gcopy[i].start()
        for h in range(i * step, (i + 1) * step):
            acopy[h].start()
    gt[:, 0:flat] = jnp.zeros((3 * cols, flat), bf16)
    gt[:, (height + 1) * flat : (height + 2) * flat] = jnp.zeros((3 * cols, flat), bf16)
    column = lax.broadcasted_iota(jnp.int32, (cols, flat), 1) % width
    is_last, is_first = column == width - 1, column == 0

    def prepare(i):
        gcopy[i].wait()
        for h in range(i * step, (i + 1) * step):
            g = gv[:, h].reshape(flat, cols).astype(f32).T
            here = slice((h + 1) * flat, (h + 2) * flat)
            gt[0:cols, here] = jnp.where(is_last, 0.0, pltpu.roll(g, flat - 1, 1)).astype(bf16)
            gt[cols : 2 * cols, here] = g.astype(bf16)
            gt[2 * cols : 3 * cols, here] = jnp.where(is_first, 0.0, pltpu.roll(g, 1, 1)).astype(bf16)

    prepare(0)
    for i in range(STEPS):
        for h in range(i * step, (i + 1) * step):
            acopy[h].wait()
        if i + 1 < STEPS:
            prepare(i + 1)
        rhs = av[i * step : (i + 1) * step].reshape(step * flat, cin)
        term = jnp.dot(gt[:, (i * step + 1) * flat : ((i + 1) * step + 1) * flat], rhs, preferred_element_type=f32)
        acc[...] = term if i == 0 else acc[...] + term
    emit(acc, turned, outs, osem, me_ref[0], cols)


def next_kernel(shift, parts, me_ref, gt, av, *rest):
    outs = rest[:parts]
    acc, turned, osem = rest[parts:]
    height, batch, width, cin = av.shape
    flat = batch * width
    cols = gt.shape[0] // 3
    lhs = gt[:, (1 + shift) * flat : (1 + shift + height) * flat]
    acc[...] = jnp.dot(lhs, av[...].reshape(height * flat, cin), preferred_element_type=f32)
    emit(acc, turned, outs, osem, me_ref[0], cols)


def conv_first(a, g, me, parts):
    batch, height, width, cin = a.shape
    cols = g.shape[3]
    flat = batch * width
    res = pl.pallas_call(
        functools.partial(first_kernel, parts),
        out_shape=[jax.ShapeDtypeStruct((3, cin // parts, cols), f32)] * parts
        + [pltpu.VMEM((height, batch, width, cin), bf16), pltpu.VMEM((3 * cols, (height + 2) * flat), bf16)],
        in_specs=[SM, HB, HB],
        out_specs=[HB] * parts + [VM, VM],
        scratch_shapes=[
            pltpu.VMEM((batch, height, width, cols), bf16),
            pltpu.VMEM((3 * cols, cin), f32),
            pltpu.VMEM((3, cin, cols), f32),
            pltpu.SemaphoreType.DMA((height,)),
            pltpu.SemaphoreType.DMA((STEPS,)),
            pltpu.SemaphoreType.DMA((parts,)),
        ],
        compiler_params=pltpu.CompilerParams(vmem_limit_bytes=FIRST_VMEM),
        cost_estimate=pl.CostEstimate(flops=6 * cols * cin * height * flat, bytes_accessed=2 * (a.size + g.size), transcendentals=0),
        name="conv_first",
    )(me, g, a)
    return list(res[:parts]), res[parts], res[parts + 1]


def conv_next(av, gt, me, shift, parts):
    height, batch, width, cin = av.shape
    cols = gt.shape[0] // 3
    return list(pl.pallas_call(
        functools.partial(next_kernel, shift, parts),
        out_shape=[jax.ShapeDtypeStruct((3, cin // parts, cols), f32)] * parts,
        in_specs=[SM, VM, VM],
        out_specs=[HB] * parts,
        scratch_shapes=[pltpu.VMEM((3 * cols, cin), f32), pltpu.VMEM((3, cin, cols), f32), pltpu.SemaphoreType.DMA((parts,))],
        compiler_params=pltpu.CompilerParams(vmem_limit_bytes=NEXT_VMEM),
        cost_estimate=pl.CostEstimate(flops=6 * cols * cin * height * batch * width, bytes_accessed=12 * cin * cols, transcendentals=0),
        name="conv_next",
    )(me, gt, av))


def tile_terms(gt, rhs, lo, hi, flat, i):
    return jnp.dot(gt[:, (lo + 2 - i) * flat : (hi + 2 - i) * flat], rhs, preferred_element_type=f32)


def tile_columns(av, chip, tiles, lo, hi):
    _, batch, width, cin = av.shape
    lanes = cin // 4
    firsts = [pl.multiple_of(jnp.bitwise_xor(chip, q) * lanes, lanes) for q in tiles]
    return jnp.concatenate([av[lo:hi, :, :, pl.ds(f, lanes)].reshape((hi - lo) * batch * width, lanes) for f in firsts], axis=1)


def tile_store(value, i, outs, me, cols):
    is_lower = jnp.bitwise_and(me, 1) == 0
    depth = outs[0].shape[0] // 9
    for q in range(len(outs) // 2):
        for j in range(3):
            turned = value[j * cols : (j + 1) * cols, q * 2 * depth : (q + 1) * 2 * depth].T
            lower, upper = turned[:depth], turned[depth:]
            here = slice((3 * i + j) * depth, (3 * i + j + 1) * depth)
            outs[2 * q][here, :] = jnp.where(is_lower, lower, upper)
            outs[2 * q + 1][here, :] = jnp.where(is_lower, upper, lower)


def near_kernel(bounds, me_ref, g_hbm, a_hbm, *rest):
    outs = rest[:4]
    av, gt, gv, acc, asem, gsem = rest[4:]
    height, batch, width, _ = av.shape
    cols = gv.shape[3]
    flat = batch * width
    rows = 3 * cols
    me = me_ref[0]
    gends = [0] + [min(b + 1, height) for b in bounds[1:]]
    gcopy = [pltpu.make_async_copy(g_hbm.at[:, h], gv.at[:, h], gsem.at[h]) for h in range(height)]
    acopy = [pltpu.make_async_copy(a_hbm.at[:, h], av.at[h], asem.at[h]) for h in range(height)]
    for copy in gcopy[: gends[1]] + acopy[: bounds[1]] + gcopy[gends[1] :] + acopy[bounds[1] :]:
        copy.start()
    gt[:, 0:flat] = jnp.zeros((rows, flat), bf16)
    gt[:, (height + 1) * flat : (height + 2) * flat] = jnp.zeros((rows, flat), bf16)
    column = lax.broadcasted_iota(jnp.int32, (cols, flat), 1) % width
    is_last, is_first = column == width - 1, column == 0

    def prepare(lo, hi):
        for h in range(lo, hi):
            g = gv[:, h].reshape(flat, cols).astype(f32).T
            here = slice((h + 1) * flat, (h + 2) * flat)
            gt[0:cols, here] = jnp.where(is_last, 0.0, pltpu.roll(g, flat - 1, 1)).astype(bf16)
            gt[cols : 2 * cols, here] = g.astype(bf16)
            gt[2 * cols : 3 * cols, here] = jnp.where(is_first, 0.0, pltpu.roll(g, 1, 1)).astype(bf16)

    for h in range(gends[1]):
        gcopy[h].wait()

    @pl.when(me >= 0)
    def _():
        prepare(0, gends[1])

    for n in range(len(bounds) - 1):
        lo, hi = bounds[n], bounds[n + 1]
        for h in range(lo, hi):
            acopy[h].wait()
        if n + 2 < len(bounds):
            for h in range(gends[n + 1], gends[n + 2]):
                gcopy[h].wait()

        @pl.when(me >= 0)
        def _(n=n, lo=lo, hi=hi):
            is_end = n + 2 == len(bounds)
            if not is_end:
                prepare(gends[n + 1], gends[n + 2])
            rhs = tile_columns(av, me // 2, (1 + jnp.bitwise_and(me, 1), 2 - jnp.bitwise_and(me, 1)), lo, hi)
            for i in range(3):
                here = slice(i * rows, (i + 1) * rows)
                term = tile_terms(gt, rhs, lo, hi, flat, i)
                if n > 0:
                    term = acc[here, :] + term
                if is_end:
                    tile_store(term, i, outs, me, cols)
                else:
                    acc[here, :] = term


def far_kernel(me_ref, gt, av, *outs):
    height, batch, width, _ = av.shape
    me = me_ref[0]
    rhs = tile_columns(av, me // 2, (3, 0), 0, height)
    for i in range(3):
        tile_store(tile_terms(gt, rhs, 0, height, batch * width, i), i, outs, me, gt.shape[0] // 3)


def near_blocks(a, g, me):
    batch, height, width, cin = a.shape
    cols = g.shape[3]
    lanes, flat = cin // 4, batch * width
    block = jax.ShapeDtypeStruct((9 * (lanes // 2), cols), f32)
    res = pl.pallas_call(
        functools.partial(near_kernel, [0, height // 8, height * 3 // 8, height * 11 // 16, height]),
        out_shape=[block] * 4 + [pltpu.VMEM((height, batch, width, cin), bf16), pltpu.VMEM((3 * cols, (height + 2) * flat), bf16)],
        in_specs=[SM, HB, HB],
        out_specs=[VM] * 6,
        scratch_shapes=[
            pltpu.VMEM((batch, height, width, cols), bf16),
            pltpu.VMEM((9 * cols, 2 * lanes), f32),
            pltpu.SemaphoreType.DMA((height,)),
            pltpu.SemaphoreType.DMA((height,)),
        ],
        compiler_params=pltpu.CompilerParams(vmem_limit_bytes=NEAR_VMEM),
        cost_estimate=pl.CostEstimate(flops=36 * cols * lanes * height * flat, bytes_accessed=2 * (a.size + g.size), transcendentals=0),
        name="conv_near",
    )(me, g, a)
    return list(res[:4]), res[4], res[5]


def far_blocks(av, gt, me):
    height, batch, width, cin = av.shape
    lanes = cin // 4
    cols = gt.shape[0] // 3
    block = jax.ShapeDtypeStruct((9 * (lanes // 2), cols), f32)
    return list(pl.pallas_call(
        far_kernel,
        out_shape=[block] * 4,
        in_specs=[SM, VM, VM],
        out_specs=[VM] * 4,
        compiler_params=pltpu.CompilerParams(vmem_limit_bytes=NEXT_VMEM),
        cost_estimate=pl.CostEstimate(flops=36 * cols * lanes * height * batch * width, bytes_accessed=72 * lanes * cols, transcendentals=0),
        name="conv_far",
    )(me, gt, av))


def gram_kernel(pairs, parts, devices, ids, *rest):
    blocks, out, rowsums = rest[:-2], rest[-2], rest[-1]
    chunks = len(blocks) // parts
    before = blocks[chunks * parts :]
    length, cols = blocks[0].shape
    rowsums[...] = jnp.zeros_like(rowsums)
    for first in range(0, len(pairs), 16):
        some = pairs[first : first + 16]
        names = sorted({n for pair in some for n in pair})
        sums = [jnp.zeros((8, cols), f32) for _ in some]
        for c in range(chunks):
            def body(i, sums):
                here = pl.ds(pl.multiple_of(i * 8, 8), 8)
                x = {k: blocks[c * parts + k][here, :] for k in names}
                return [s + x[k] * x[l] for s, (k, l) in zip(sums, some)]

            sums = lax.fori_loop(0, length // 8, body, sums, unroll=8)
        for s, (k, l) in zip(sums, some):
            rowsums[k * parts + l : k * parts + l + 1, :] = jnp.sum(s, axis=0, keepdims=True)
    number = lax.broadcasted_iota(jnp.int32, (parts * parts, 128), 0)
    a, b = jnp.zeros_like(number), jnp.zeros_like(number)
    for k in range(parts):
        a = jnp.where(number // parts == k, ids[k], a)
        b = jnp.where(number % parts == k, ids[k], b)
    at = jnp.minimum(a, b) * parts + jnp.maximum(a, b)
    place = lax.broadcasted_iota(jnp.int32, (parts * parts, 128), 1)
    values = jnp.sum(rowsums[...], axis=1, keepdims=True)
    for r in range(out.shape[-2]):
        total = jnp.sum(jnp.where(at == place + r * 128, values, 0.0), axis=0, keepdims=True)
        for part in before:
            total = total + part[r : r + 1, :]
        for n in range(max(devices, 1)):
            if devices:
                out[n, r : r + 1, :] = total
            else:
                out[r : r + 1, :] = total


def gram(chunks, pairs, before, ids, devices):
    parts = len(chunks[0])
    rows = -(-parts * parts // 128)
    shape = (devices, rows, 128) if devices else (rows, 128)
    flat = [b for chunk in chunks for b in chunk]
    return pl.pallas_call(
        functools.partial(gram_kernel, pairs, parts, devices),
        out_shape=jax.ShapeDtypeStruct(shape, f32),
        in_specs=[SM] + [VM] * (len(flat) + len(before)),
        out_specs=VM,
        scratch_shapes=[pltpu.VMEM((parts * parts, flat[0].shape[1]), f32)],
        compiler_params=pltpu.CompilerParams(vmem_limit_bytes=NEXT_VMEM),
        cost_estimate=pl.CostEstimate(flops=2 * flat[0].size * len(chunks) * len(pairs), bytes_accessed=4 * flat[0].size * len(flat), transcendentals=0),
        name="gram",
    )(ids, *flat, *before)


def mixes_of(sums, parts):
    rows = sums.shape[0]
    place = lax.broadcasted_iota(jnp.int32, (rows, 128), 0) * 128 + lax.broadcasted_iota(jnp.int32, (rows, 128), 1)
    g = {}
    for a in range(parts):
        for b in range(a, parts):
            g[a, b] = g[b, a] = jnp.sum(jnp.where(place == a * parts + b, sums, 0.0), axis=(0, 1), keepdims=True)
    factors = [None] * parts
    count, width = parts, 1
    while count > 1:
        coef = []
        for k in range(count // 2):
            p, qa, qb = g[2 * k, 2 * k + 1], g[2 * k, 2 * k] + 1e-6, g[2 * k + 1, 2 * k + 1] + 1e-6
            coef += [1.0 - p / (2.0 * qa), 1.0 - p / (2.0 * qb)]
        for r in range(parts):
            c = coef[r // width]
            factors[r] = c if factors[r] is None else factors[r] * c
        count, width = count // 2, width * 2
        new = {}
        for k in range(count):
            for l in range(k, count):
                new[k, l] = new[l, k] = sum(coef[x] * coef[y] * g[x, y] for x in (2 * k, 2 * k + 1) for y in (2 * l, 2 * l + 1))
        g = new
    return factors


def final_kernel(parts, ids, sums, weight, momentum, *rest):
    blocks, (new_weight, new_momentum) = rest[:-2], rest[-2:]
    total = jnp.sum(sums[...], axis=0)
    factors = mixes_of(total, parts)
    mine = []
    for k in range(parts):
        pick = factors[0]
        for r in range(1, parts):
            pick = jnp.where(ids[k] == r, factors[r], pick)
        mine.append(pick)
    length = blocks[0].shape[0]
    for c in range(len(blocks) // parts):
        here = slice(c * length, (c + 1) * length)
        value = 0.9 * momentum[here, :]
        for k in range(parts):
            value = value + mine[k] * blocks[c * parts + k][...]
        new_momentum[here, :] = value
        new_weight[here, :] = weight[here, :] - 0.1 * value


def finish(sums, weight, momentum, chunks, ids):
    parts = len(chunks[0])
    depth, cols = weight.shape[0], weight.shape[3]
    w, m = (jnp.transpose(x, (1, 2, 0, 3)).reshape(9 * depth, cols) for x in (weight, momentum))
    flat = [b for chunk in chunks for b in chunk]
    outs = pl.pallas_call(
        functools.partial(final_kernel, parts),
        out_shape=[jax.ShapeDtypeStruct(w.shape, f32)] * 2,
        in_specs=[SM] + [VM] * (3 + len(flat)),
        out_specs=[VM, VM],
        compiler_params=pltpu.CompilerParams(vmem_limit_bytes=NEXT_VMEM),
        cost_estimate=pl.CostEstimate(flops=2 * w.size * parts, bytes_accessed=4 * w.size * (parts + 4), transcendentals=0),
        name="final",
    )(ids, sums, w, m, *flat)
    return tuple(jnp.transpose(x.reshape(3, 3, depth, cols), (2, 0, 1, 3)) for x in outs)


def upper_pairs(parts):
    return [(k, l) for k in range(parts) for l in range(k, parts)]


def send(block, parts, flips):
    return lax.ppermute(block, "dp", [(r, r ^ flips[r % 2]) for r in range(parts)])


def by_rows(activations, out_grads, me, parts):
    def exchange(blocks):
        blocks = [b.reshape(-1, b.shape[2]) for b in blocks]
        return blocks[:1] + [send(blocks[k], parts, (k, k)) for k in range(1, parts)]

    middle, av, gt = conv_first(activations, out_grads, me, parts)
    middle = exchange(middle)
    lower = exchange(conv_next(av, gt, me, 1, parts))
    upper = exchange(conv_next(av, gt, me, -1, parts))
    return [lower, middle, upper], upper_pairs(parts), [], jnp.bitwise_xor(me, jnp.arange(parts, dtype=jnp.int32))


def by_chips(activations, out_grads, me, parts):
    flips = [(2, 4), (3, 5), (4, 2), (5, 3)]
    near, av, gt = near_blocks(activations, out_grads, me)
    near = [send(block, parts, flip) for block, flip in zip(near, flips)]
    far = far_blocks(av, gt, me)
    far = [send(far[k], parts, (6 + k, 6 + k)) for k in range(2)] + [far[2], send(far[3], parts, (1, 1))]
    even = jnp.array([0, 1, 2, 5, 4, 3, 6, 7], jnp.int32)
    odd = jnp.array([0, 1, 4, 3, 2, 5, 6, 7], jnp.int32)
    ids = jnp.bitwise_xor(me, jnp.where(me % 2 == 0, even, odd))
    blocks = far[2:] + near + far[:2]
    early = [pair for pair in upper_pairs(parts) if pair[1] < EARLY]
    partial = gram([blocks[:EARLY] + [blocks[0]] * (parts - EARLY)], early, [], ids, 0)
    return [blocks], [pair for pair in upper_pairs(parts) if pair[1] >= EARLY], [partial], ids


def shards(activations, out_grads, weight, momentum):
    parts = lax.axis_size("dp")
    devices = parts * lax.axis_size("chan")
    me = lax.axis_index("dp").reshape(1).astype(jnp.int32)
    four = parts == 8 and activations.shape[3] % 512 == 0
    chunks, pairs, before, ids = (by_chips if four else by_rows)(activations, out_grads, me, parts)
    sums = gram(chunks, pairs, before, ids, devices)
    sums = lax.all_to_all(sums, ("dp", "chan"), split_axis=0, concat_axis=0, tiled=True)
    return finish(sums, weight, momentum, chunks, ids)


EARLY = 4
FIRST_VMEM, NEXT_VMEM, NEAR_VMEM = 30 << 20, 30 << 20, 38 << 20


def solution(mesh):
    in_specs = (
        P("dp", None, None, None),
        P("dp", None, None, "chan"),
        P("dp", None, None, "chan"),
        P("dp", None, None, "chan"),
    )
    out_specs = (P("dp", None, None, "chan"), P("dp", None, None, "chan"))
    return jax.shard_map(shards, mesh=mesh, in_specs=in_specs, out_specs=out_specs, check_vma=False)
```

```python
import functools

import jax
import jax.numpy as jnp
from jax import lax
from jax.experimental import pallas as pl
from jax.experimental.pallas import tpu as pltpu
from jax.sharding import PartitionSpec as P


f32, bf16 = jnp.float32, jnp.bfloat16
SM = pl.BlockSpec(memory_space=pltpu.SMEM)
VM = pl.BlockSpec(memory_space=pltpu.VMEM)
HB = pl.BlockSpec(memory_space=pltpu.HBM)
STEPS = 8


def emit(acc, turned, outs, sem, me, cols):
    rows = turned.shape[1] // len(outs)
    for j in range(3):
        turned[j] = acc[j * cols : (j + 1) * cols, :].T
    copies = []
    for k, out in enumerate(outs):
        first = pl.multiple_of(jnp.bitwise_xor(me, k) * rows, rows)
        copies.append(pltpu.make_async_copy(turned.at[:, pl.ds(first, rows), :], out, sem.at[k]))
    for copy in copies:
        copy.start()
    for copy in copies:
        copy.wait()


def first_kernel(parts, me_ref, g_hbm, a_hbm, *rest):
    outs = rest[:parts]
    av, gt, gv, acc, turned, asem, gsem, osem = rest[parts:]
    height, batch, width, cin = av.shape
    cols = gv.shape[3]
    flat = batch * width
    step = height // STEPS
    acopy = [pltpu.make_async_copy(a_hbm.at[:, h], av.at[h], asem.at[h]) for h in range(height)]
    gcopy = [pltpu.make_async_copy(g_hbm.at[:, i * step : (i + 1) * step], gv.at[:, i * step : (i + 1) * step], gsem.at[i]) for i in range(STEPS)]
    for i in range(STEPS):
        gcopy[i].start()
        for h in range(i * step, (i + 1) * step):
            acopy[h].start()
    gt[:, 0:flat] = jnp.zeros((3 * cols, flat), bf16)
    gt[:, (height + 1) * flat : (height + 2) * flat] = jnp.zeros((3 * cols, flat), bf16)
    column = lax.broadcasted_iota(jnp.int32, (cols, flat), 1) % width
    is_last, is_first = column == width - 1, column == 0

    def prepare(i):
        gcopy[i].wait()
        for h in range(i * step, (i + 1) * step):
            g = gv[:, h].reshape(flat, cols).astype(f32).T
            here = slice((h + 1) * flat, (h + 2) * flat)
            gt[0:cols, here] = jnp.where(is_last, 0.0, pltpu.roll(g, flat - 1, 1)).astype(bf16)
            gt[cols : 2 * cols, here] = g.astype(bf16)
            gt[2 * cols : 3 * cols, here] = jnp.where(is_first, 0.0, pltpu.roll(g, 1, 1)).astype(bf16)

    prepare(0)
    for i in range(STEPS):
        for h in range(i * step, (i + 1) * step):
            acopy[h].wait()
        if i + 1 < STEPS:
            prepare(i + 1)
        rhs = av[i * step : (i + 1) * step].reshape(step * flat, cin)
        term = jnp.dot(gt[:, (i * step + 1) * flat : ((i + 1) * step + 1) * flat], rhs, preferred_element_type=f32)
        acc[...] = term if i == 0 else acc[...] + term
    emit(acc, turned, outs, osem, me_ref[0], cols)


def next_kernel(shift, parts, me_ref, gt, av, *rest):
    outs = rest[:parts]
    acc, turned, osem = rest[parts:]
    height, batch, width, cin = av.shape
    flat = batch * width
    cols = gt.shape[0] // 3
    lhs = gt[:, (1 + shift) * flat : (1 + shift + height) * flat]
    acc[...] = jnp.dot(lhs, av[...].reshape(height * flat, cin), preferred_element_type=f32)
    emit(acc, turned, outs, osem, me_ref[0], cols)


def conv_first(a, g, me, parts):
    batch, height, width, cin = a.shape
    cols = g.shape[3]
    flat = batch * width
    res = pl.pallas_call(
        functools.partial(first_kernel, parts),
        out_shape=[jax.ShapeDtypeStruct((3, cin // parts, cols), f32)] * parts
        + [pltpu.VMEM((height, batch, width, cin), bf16), pltpu.VMEM((3 * cols, (height + 2) * flat), bf16)],
        in_specs=[SM, HB, HB],
        out_specs=[HB] * parts + [VM, VM],
        scratch_shapes=[
            pltpu.VMEM((batch, height, width, cols), bf16),
            pltpu.VMEM((3 * cols, cin), f32),
            pltpu.VMEM((3, cin, cols), f32),
            pltpu.SemaphoreType.DMA((height,)),
            pltpu.SemaphoreType.DMA((STEPS,)),
            pltpu.SemaphoreType.DMA((parts,)),
        ],
        compiler_params=pltpu.CompilerParams(vmem_limit_bytes=FIRST_VMEM),
        cost_estimate=pl.CostEstimate(flops=6 * cols * cin * height * flat, bytes_accessed=2 * (a.size + g.size), transcendentals=0),
        name="conv_first",
    )(me, g, a)
    return list(res[:parts]), res[parts], res[parts + 1]


def conv_next(av, gt, me, shift, parts):
    height, batch, width, cin = av.shape
    cols = gt.shape[0] // 3
    return list(pl.pallas_call(
        functools.partial(next_kernel, shift, parts),
        out_shape=[jax.ShapeDtypeStruct((3, cin // parts, cols), f32)] * parts,
        in_specs=[SM, VM, VM],
        out_specs=[HB] * parts,
        scratch_shapes=[pltpu.VMEM((3 * cols, cin), f32), pltpu.VMEM((3, cin, cols), f32), pltpu.SemaphoreType.DMA((parts,))],
        compiler_params=pltpu.CompilerParams(vmem_limit_bytes=NEXT_VMEM),
        cost_estimate=pl.CostEstimate(flops=6 * cols * cin * height * batch * width, bytes_accessed=12 * cin * cols, transcendentals=0),
        name="conv_next",
    )(me, gt, av))


def tile_terms(gt, rhs, lo, hi, flat, i):
    return jnp.dot(gt[:, (lo + 2 - i) * flat : (hi + 2 - i) * flat], rhs, preferred_element_type=f32)


def tile_columns(av, chip, tiles, lo, hi):
    _, batch, width, cin = av.shape
    lanes = cin // 4
    firsts = [pl.multiple_of(jnp.bitwise_xor(chip, q) * lanes, lanes) for q in tiles]
    return jnp.concatenate([av[lo:hi, :, :, pl.ds(f, lanes)].reshape((hi - lo) * batch * width, lanes) for f in firsts], axis=1)


def tile_store(value, i, outs, me, cols):
    is_lower = jnp.bitwise_and(me, 1) == 0
    depth = outs[0].shape[0] // 9
    for q in range(len(outs) // 2):
        for j in range(3):
            turned = value[j * cols : (j + 1) * cols, q * 2 * depth : (q + 1) * 2 * depth].T
            lower, upper = turned[:depth], turned[depth:]
            here = slice((3 * i + j) * depth, (3 * i + j + 1) * depth)
            outs[2 * q][here, :] = jnp.where(is_lower, lower, upper)
            outs[2 * q + 1][here, :] = jnp.where(is_lower, upper, lower)


def near_kernel(bounds, me_ref, g_hbm, a_hbm, *rest):
    outs = rest[:4]
    av, gt, gv, acc, asem, gsem = rest[4:]
    height, batch, width, _ = av.shape
    cols = gv.shape[3]
    flat = batch * width
    rows = 3 * cols
    me = me_ref[0]
    gends = [0] + [min(b + 1, height) for b in bounds[1:]]
    gcopy = [pltpu.make_async_copy(g_hbm.at[:, h], gv.at[:, h], gsem.at[h]) for h in range(height)]
    acopy = [pltpu.make_async_copy(a_hbm.at[:, h], av.at[h], asem.at[h]) for h in range(height)]
    for copy in gcopy[: gends[1]] + acopy[: bounds[1]] + gcopy[gends[1] :] + acopy[bounds[1] :]:
        copy.start()
    gt[:, 0:flat] = jnp.zeros((rows, flat), bf16)
    gt[:, (height + 1) * flat : (height + 2) * flat] = jnp.zeros((rows, flat), bf16)
    column = lax.broadcasted_iota(jnp.int32, (cols, flat), 1) % width
    is_last, is_first = column == width - 1, column == 0

    def prepare(lo, hi):
        for h in range(lo, hi):
            g = gv[:, h].reshape(flat, cols).astype(f32).T
            here = slice((h + 1) * flat, (h + 2) * flat)
            gt[0:cols, here] = jnp.where(is_last, 0.0, pltpu.roll(g, flat - 1, 1)).astype(bf16)
            gt[cols : 2 * cols, here] = g.astype(bf16)
            gt[2 * cols : 3 * cols, here] = jnp.where(is_first, 0.0, pltpu.roll(g, 1, 1)).astype(bf16)

    for h in range(gends[1]):
        gcopy[h].wait()

    @pl.when(me >= 0)
    def _():
        prepare(0, gends[1])

    for n in range(len(bounds) - 1):
        lo, hi = bounds[n], bounds[n + 1]
        for h in range(lo, hi):
            acopy[h].wait()
        if n + 2 < len(bounds):
            for h in range(gends[n + 1], gends[n + 2]):
                gcopy[h].wait()

        @pl.when(me >= 0)
        def _(n=n, lo=lo, hi=hi):
            is_end = n + 2 == len(bounds)
            if not is_end:
                prepare(gends[n + 1], gends[n + 2])
            rhs = tile_columns(av, me // 2, (1 + jnp.bitwise_and(me, 1), 2 - jnp.bitwise_and(me, 1)), lo, hi)
            for i in range(3):
                here = slice(i * rows, (i + 1) * rows)
                term = tile_terms(gt, rhs, lo, hi, flat, i)
                if n > 0:
                    term = acc[here, :] + term
                if is_end:
                    tile_store(term, i, outs, me, cols)
                else:
                    acc[here, :] = term


def far_kernel(me_ref, gt, av, *outs):
    height, batch, width, _ = av.shape
    me = me_ref[0]
    rhs = tile_columns(av, me // 2, (3, 0), 0, height)
    for i in range(3):
        tile_store(tile_terms(gt, rhs, 0, height, batch * width, i), i, outs, me, gt.shape[0] // 3)


def near_blocks(a, g, me):
    batch, height, width, cin = a.shape
    cols = g.shape[3]
    lanes, flat = cin // 4, batch * width
    block = jax.ShapeDtypeStruct((9 * (lanes // 2), cols), f32)
    res = pl.pallas_call(
        functools.partial(near_kernel, [0, height // 8, height * 3 // 8, height * 11 // 16, height]),
        out_shape=[block] * 4 + [pltpu.VMEM((height, batch, width, cin), bf16), pltpu.VMEM((3 * cols, (height + 2) * flat), bf16)],
        in_specs=[SM, HB, HB],
        out_specs=[VM] * 6,
        scratch_shapes=[
            pltpu.VMEM((batch, height, width, cols), bf16),
            pltpu.VMEM((9 * cols, 2 * lanes), f32),
            pltpu.SemaphoreType.DMA((height,)),
            pltpu.SemaphoreType.DMA((height,)),
        ],
        compiler_params=pltpu.CompilerParams(vmem_limit_bytes=NEAR_VMEM),
        cost_estimate=pl.CostEstimate(flops=36 * cols * lanes * height * flat, bytes_accessed=2 * (a.size + g.size), transcendentals=0),
        name="conv_near",
    )(me, g, a)
    return list(res[:4]), res[4], res[5]


def far_blocks(av, gt, me):
    height, batch, width, cin = av.shape
    lanes = cin // 4
    cols = gt.shape[0] // 3
    block = jax.ShapeDtypeStruct((9 * (lanes // 2), cols), f32)
    return list(pl.pallas_call(
        far_kernel,
        out_shape=[block] * 4,
        in_specs=[SM, VM, VM],
        out_specs=[VM] * 4,
        compiler_params=pltpu.CompilerParams(vmem_limit_bytes=NEXT_VMEM),
        cost_estimate=pl.CostEstimate(flops=36 * cols * lanes * height * batch * width, bytes_accessed=72 * lanes * cols, transcendentals=0),
        name="conv_far",
    )(me, gt, av))


def gram_kernel(pairs, parts, devices, ids, *rest):
    blocks, out, rowsums = rest[:-2], rest[-2], rest[-1]
    chunks = len(blocks) // parts
    before = blocks[chunks * parts :]
    length, cols = blocks[0].shape
    rowsums[...] = jnp.zeros_like(rowsums)
    for first in range(0, len(pairs), 16):
        some = pairs[first : first + 16]
        names = sorted({n for pair in some for n in pair})
        sums = [jnp.zeros((8, cols), f32) for _ in some]
        for c in range(chunks):
            def body(i, sums):
                here = pl.ds(pl.multiple_of(i * 8, 8), 8)
                x = {k: blocks[c * parts + k][here, :] for k in names}
                return [s + x[k] * x[l] for s, (k, l) in zip(sums, some)]

            sums = lax.fori_loop(0, length // 8, body, sums, unroll=8)
        for s, (k, l) in zip(sums, some):
            rowsums[k * parts + l : k * parts + l + 1, :] = jnp.sum(s, axis=0, keepdims=True)
    number = lax.broadcasted_iota(jnp.int32, (parts * parts, 128), 0)
    a, b = jnp.zeros_like(number), jnp.zeros_like(number)
    for k in range(parts):
        a = jnp.where(number // parts == k, ids[k], a)
        b = jnp.where(number % parts == k, ids[k], b)
    at = jnp.minimum(a, b) * parts + jnp.maximum(a, b)
    place = lax.broadcasted_iota(jnp.int32, (parts * parts, 128), 1)
    values = jnp.sum(rowsums[...], axis=1, keepdims=True)
    for r in range(out.shape[-2]):
        total = jnp.sum(jnp.where(at == place + r * 128, values, 0.0), axis=0, keepdims=True)
        for part in before:
            total = total + part[r : r + 1, :]
        for n in range(max(devices, 1)):
            if devices:
                out[n, r : r + 1, :] = total
            else:
                out[r : r + 1, :] = total


def gram(chunks, pairs, before, ids, devices):
    parts = len(chunks[0])
    rows = -(-parts * parts // 128)
    shape = (devices, rows, 128) if devices else (rows, 128)
    flat = [b for chunk in chunks for b in chunk]
    return pl.pallas_call(
        functools.partial(gram_kernel, pairs, parts, devices),
        out_shape=jax.ShapeDtypeStruct(shape, f32),
        in_specs=[SM] + [VM] * (len(flat) + len(before)),
        out_specs=VM,
        scratch_shapes=[pltpu.VMEM((parts * parts, flat[0].shape[1]), f32)],
        compiler_params=pltpu.CompilerParams(vmem_limit_bytes=NEXT_VMEM),
        cost_estimate=pl.CostEstimate(flops=2 * flat[0].size * len(chunks) * len(pairs), bytes_accessed=4 * flat[0].size * len(flat), transcendentals=0),
        name="gram",
    )(ids, *flat, *before)


def mixes_of(sums, parts):
    rows = sums.shape[0]
    place = lax.broadcasted_iota(jnp.int32, (rows, 128), 0) * 128 + lax.broadcasted_iota(jnp.int32, (rows, 128), 1)
    g = {}
    for a in range(parts):
        for b in range(a, parts):
            g[a, b] = g[b, a] = jnp.sum(jnp.where(place == a * parts + b, sums, 0.0), axis=(0, 1), keepdims=True)
    factors = [None] * parts
    count, width = parts, 1
    while count > 1:
        coef = []
        for k in range(count // 2):
            p, qa, qb = g[2 * k, 2 * k + 1], g[2 * k, 2 * k] + 1e-6, g[2 * k + 1, 2 * k + 1] + 1e-6
            coef += [1.0 - p / (2.0 * qa), 1.0 - p / (2.0 * qb)]
        for r in range(parts):
            c = coef[r // width]
            factors[r] = c if factors[r] is None else factors[r] * c
        count, width = count // 2, width * 2
        new = {}
        for k in range(count):
            for l in range(k, count):
                new[k, l] = new[l, k] = sum(coef[x] * coef[y] * g[x, y] for x in (2 * k, 2 * k + 1) for y in (2 * l, 2 * l + 1))
        g = new
    return factors


def final_kernel(parts, ids, sums, weight, momentum, *rest):
    blocks, (new_weight, new_momentum) = rest[:-2], rest[-2:]
    total = jnp.sum(sums[...], axis=0)
    factors = mixes_of(total, parts)
    mine = []
    for k in range(parts):
        pick = factors[0]
        for r in range(1, parts):
            pick = jnp.where(ids[k] == r, factors[r], pick)
        mine.append(pick)
    length = blocks[0].shape[0]
    size = length // 3
    for n in range(3 * (len(blocks) // parts)):
        for r in range(0, size, 64):
            end = min(r + 64, size)
            here, there = slice(n * size + r, n * size + end), slice(n % 3 * size + r, n % 3 * size + end)
            value = 0.9 * momentum[here, :]
            for k in range(parts):
                value = value + mine[k] * blocks[n // 3 * parts + k][there, :]
            new_momentum[here, :] = value
            new_weight[here, :] = weight[here, :] - 0.1 * value


def finish(sums, weight, momentum, chunks, ids):
    parts = len(chunks[0])
    depth, cols = weight.shape[0], weight.shape[3]
    w, m = (jnp.transpose(x, (1, 2, 0, 3)).reshape(9 * depth, cols) for x in (weight, momentum))
    flat = [b for chunk in chunks for b in chunk]
    outs = pl.pallas_call(
        functools.partial(final_kernel, parts),
        out_shape=[jax.ShapeDtypeStruct(w.shape, f32)] * 2,
        in_specs=[SM] + [VM] * (3 + len(flat)),
        out_specs=[VM, VM],
        compiler_params=pltpu.CompilerParams(vmem_limit_bytes=NEXT_VMEM),
        cost_estimate=pl.CostEstimate(flops=2 * w.size * parts, bytes_accessed=4 * w.size * (parts + 4), transcendentals=0),
        name="final",
    )(ids, sums, w, m, *flat)
    return tuple(jnp.transpose(x.reshape(3, 3, depth, cols), (2, 0, 1, 3)) for x in outs)


def upper_pairs(parts):
    return [(k, l) for k in range(parts) for l in range(k, parts)]


def send(block, parts, flips):
    return lax.ppermute(block, "dp", [(r, r ^ flips[r % 2]) for r in range(parts)])


def by_rows(activations, out_grads, me, parts):
    def exchange(blocks):
        blocks = [b.reshape(-1, b.shape[2]) for b in blocks]
        return blocks[:1] + [send(blocks[k], parts, (k, k)) for k in range(1, parts)]

    middle, av, gt = conv_first(activations, out_grads, me, parts)
    middle = exchange(middle)
    lower = exchange(conv_next(av, gt, me, 1, parts))
    upper = exchange(conv_next(av, gt, me, -1, parts))
    return [lower, middle, upper], upper_pairs(parts), [], jnp.bitwise_xor(me, jnp.arange(parts, dtype=jnp.int32))


def by_chips(activations, out_grads, me, parts):
    flips = [(2, 4), (3, 5), (4, 2), (5, 3)]
    near, av, gt = near_blocks(activations, out_grads, me)
    near = [send(block, parts, flip) for block, flip in zip(near, flips)]
    far = far_blocks(av, gt, me)
    far = [send(far[k], parts, (6 + k, 6 + k)) for k in range(2)] + [far[2], send(far[3], parts, (1, 1))]
    even = jnp.array([0, 1, 2, 5, 4, 3, 6, 7], jnp.int32)
    odd = jnp.array([0, 1, 4, 3, 2, 5, 6, 7], jnp.int32)
    ids = jnp.bitwise_xor(me, jnp.where(me % 2 == 0, even, odd))
    blocks = far[2:] + near + far[:2]
    partials, first = [], 0
    for last in (parts - 2, parts - 1):
        pairs = [pair for pair in upper_pairs(parts) if first <= pair[1] < last]
        partials = [gram([blocks[:last] + [blocks[0]] * (parts - last)], pairs, partials, ids, 0)]
        first = last
    return [blocks], [pair for pair in upper_pairs(parts) if pair[1] >= first], partials, ids


def shards(activations, out_grads, weight, momentum):
    parts = lax.axis_size("dp")
    devices = parts * lax.axis_size("chan")
    me = lax.axis_index("dp").reshape(1).astype(jnp.int32)
    four = parts == 8 and activations.shape[3] % 512 == 0
    chunks, pairs, before, ids = (by_chips if four else by_rows)(activations, out_grads, me, parts)
    sums = gram(chunks, pairs, before, ids, devices)
    sums = lax.all_to_all(sums, ("dp", "chan"), split_axis=0, concat_axis=0, tiled=True)
    return finish(sums, weight, momentum, chunks, ids)


FIRST_VMEM, NEXT_VMEM, NEAR_VMEM = 30 << 20, 30 << 20, 38 << 20


def solution(mesh):
    in_specs = (
        P("dp", None, None, None),
        P("dp", None, None, "chan"),
        P("dp", None, None, "chan"),
        P("dp", None, None, "chan"),
    )
    out_specs = (P("dp", None, None, "chan"), P("dp", None, None, "chan"))
    return jax.shard_map(shards, mesh=mesh, in_specs=in_specs, out_specs=out_specs, check_vma=False)
```

```python
import functools

import jax
import jax.numpy as jnp
from jax import lax
from jax.experimental import pallas as pl
from jax.experimental.pallas import tpu as pltpu
from jax.sharding import PartitionSpec as P


f32, bf16 = jnp.float32, jnp.bfloat16
SM = pl.BlockSpec(memory_space=pltpu.SMEM)
VM = pl.BlockSpec(memory_space=pltpu.VMEM)
HB = pl.BlockSpec(memory_space=pltpu.HBM)
STEPS = 8


def emit(acc, turned, outs, sem, me, cols):
    rows = turned.shape[1] // len(outs)
    for j in range(3):
        turned[j] = acc[j * cols : (j + 1) * cols, :].T
    copies = []
    for k, out in enumerate(outs):
        first = pl.multiple_of(jnp.bitwise_xor(me, k) * rows, rows)
        copies.append(pltpu.make_async_copy(turned.at[:, pl.ds(first, rows), :], out, sem.at[k]))
    for copy in copies:
        copy.start()
    for copy in copies:
        copy.wait()


def first_kernel(parts, me_ref, g_hbm, a_hbm, *rest):
    outs = rest[:parts]
    av, gt, gv, acc, turned, asem, gsem, osem = rest[parts:]
    height, batch, width, cin = av.shape
    cols = gv.shape[3]
    flat = batch * width
    step = height // STEPS
    acopy = [pltpu.make_async_copy(a_hbm.at[:, h], av.at[h], asem.at[h]) for h in range(height)]
    gcopy = [pltpu.make_async_copy(g_hbm.at[:, i * step : (i + 1) * step], gv.at[:, i * step : (i + 1) * step], gsem.at[i]) for i in range(STEPS)]
    for i in range(STEPS):
        gcopy[i].start()
        for h in range(i * step, (i + 1) * step):
            acopy[h].start()
    gt[:, 0:flat] = jnp.zeros((3 * cols, flat), bf16)
    gt[:, (height + 1) * flat : (height + 2) * flat] = jnp.zeros((3 * cols, flat), bf16)
    column = lax.broadcasted_iota(jnp.int32, (cols, flat), 1) % width
    is_last, is_first = column == width - 1, column == 0

    def prepare(i):
        gcopy[i].wait()
        for h in range(i * step, (i + 1) * step):
            g = gv[:, h].reshape(flat, cols).astype(f32).T
            here = slice((h + 1) * flat, (h + 2) * flat)
            gt[0:cols, here] = jnp.where(is_last, 0.0, pltpu.roll(g, flat - 1, 1)).astype(bf16)
            gt[cols : 2 * cols, here] = g.astype(bf16)
            gt[2 * cols : 3 * cols, here] = jnp.where(is_first, 0.0, pltpu.roll(g, 1, 1)).astype(bf16)

    prepare(0)
    for i in range(STEPS):
        for h in range(i * step, (i + 1) * step):
            acopy[h].wait()
        if i + 1 < STEPS:
            prepare(i + 1)
        rhs = av[i * step : (i + 1) * step].reshape(step * flat, cin)
        term = jnp.dot(gt[:, (i * step + 1) * flat : ((i + 1) * step + 1) * flat], rhs, preferred_element_type=f32)
        acc[...] = term if i == 0 else acc[...] + term
    emit(acc, turned, outs, osem, me_ref[0], cols)


def next_kernel(shift, parts, me_ref, gt, av, *rest):
    outs = rest[:parts]
    acc, turned, osem = rest[parts:]
    height, batch, width, cin = av.shape
    flat = batch * width
    cols = gt.shape[0] // 3
    lhs = gt[:, (1 + shift) * flat : (1 + shift + height) * flat]
    acc[...] = jnp.dot(lhs, av[...].reshape(height * flat, cin), preferred_element_type=f32)
    emit(acc, turned, outs, osem, me_ref[0], cols)


def conv_first(a, g, me, parts):
    batch, height, width, cin = a.shape
    cols = g.shape[3]
    flat = batch * width
    res = pl.pallas_call(
        functools.partial(first_kernel, parts),
        out_shape=[jax.ShapeDtypeStruct((3, cin // parts, cols), f32)] * parts
        + [pltpu.VMEM((height, batch, width, cin), bf16), pltpu.VMEM((3 * cols, (height + 2) * flat), bf16)],
        in_specs=[SM, HB, HB],
        out_specs=[HB] * parts + [VM, VM],
        scratch_shapes=[
            pltpu.VMEM((batch, height, width, cols), bf16),
            pltpu.VMEM((3 * cols, cin), f32),
            pltpu.VMEM((3, cin, cols), f32),
            pltpu.SemaphoreType.DMA((height,)),
            pltpu.SemaphoreType.DMA((STEPS,)),
            pltpu.SemaphoreType.DMA((parts,)),
        ],
        compiler_params=pltpu.CompilerParams(vmem_limit_bytes=FIRST_VMEM),
        cost_estimate=pl.CostEstimate(flops=6 * cols * cin * height * flat, bytes_accessed=2 * (a.size + g.size), transcendentals=0),
        name="conv_first",
    )(me, g, a)
    return list(res[:parts]), res[parts], res[parts + 1]


def conv_next(av, gt, me, shift, parts):
    height, batch, width, cin = av.shape
    cols = gt.shape[0] // 3
    return list(pl.pallas_call(
        functools.partial(next_kernel, shift, parts),
        out_shape=[jax.ShapeDtypeStruct((3, cin // parts, cols), f32)] * parts,
        in_specs=[SM, VM, VM],
        out_specs=[HB] * parts,
        scratch_shapes=[pltpu.VMEM((3 * cols, cin), f32), pltpu.VMEM((3, cin, cols), f32), pltpu.SemaphoreType.DMA((parts,))],
        compiler_params=pltpu.CompilerParams(vmem_limit_bytes=NEXT_VMEM),
        cost_estimate=pl.CostEstimate(flops=6 * cols * cin * height * batch * width, bytes_accessed=12 * cin * cols, transcendentals=0),
        name="conv_next",
    )(me, gt, av))


def tile_terms(gt, rhs, lo, hi, flat, i):
    return jnp.dot(gt[:, (lo + 2 - i) * flat : (hi + 2 - i) * flat], rhs, preferred_element_type=f32)


def tile_columns(av, chip, tiles, lo, hi):
    _, batch, width, cin = av.shape
    lanes = cin // 4
    firsts = [pl.multiple_of(jnp.bitwise_xor(chip, q) * lanes, lanes) for q in tiles]
    return jnp.concatenate([av[lo:hi, :, :, pl.ds(f, lanes)].reshape((hi - lo) * batch * width, lanes) for f in firsts], axis=1)


def tile_store(value, i, taps, outs, me, cols):
    i = taps.index(i)
    is_lower = jnp.bitwise_and(me, 1) == 0
    depth = outs[0].shape[0] // (3 * len(taps))
    for q in range(len(outs) // 2):
        for j in range(3):
            turned = value[j * cols : (j + 1) * cols, q * 2 * depth : (q + 1) * 2 * depth].T
            lower, upper = turned[:depth], turned[depth:]
            here = slice((3 * i + j) * depth, (3 * i + j + 1) * depth)
            outs[2 * q][here, :] = jnp.where(is_lower, lower, upper)
            outs[2 * q + 1][here, :] = jnp.where(is_lower, upper, lower)


def near_kernel(bounds, taps, me_ref, g_hbm, a_hbm, *rest):
    outs = rest[:4]
    av, gt, gv, acc, asem, gsem = rest[4:]
    height, batch, width, _ = av.shape
    cols = gv.shape[3]
    flat = batch * width
    rows = 3 * cols
    me = me_ref[0]
    gends = [0] + [min(b + 1, height) for b in bounds[1:]]
    gcopy = [pltpu.make_async_copy(g_hbm.at[:, h], gv.at[:, h], gsem.at[h]) for h in range(height)]
    acopy = [pltpu.make_async_copy(a_hbm.at[:, h], av.at[h], asem.at[h]) for h in range(height)]
    for copy in gcopy[: gends[1]] + acopy[: bounds[1]] + gcopy[gends[1] :] + acopy[bounds[1] :]:
        copy.start()
    gt[:, 0:flat] = jnp.zeros((rows, flat), bf16)
    gt[:, (height + 1) * flat : (height + 2) * flat] = jnp.zeros((rows, flat), bf16)
    column = lax.broadcasted_iota(jnp.int32, (cols, flat), 1) % width
    is_last, is_first = column == width - 1, column == 0

    def prepare(lo, hi):
        for h in range(lo, hi):
            g = gv[:, h].reshape(flat, cols).astype(f32).T
            here = slice((h + 1) * flat, (h + 2) * flat)
            gt[0:cols, here] = jnp.where(is_last, 0.0, pltpu.roll(g, flat - 1, 1)).astype(bf16)
            gt[cols : 2 * cols, here] = g.astype(bf16)
            gt[2 * cols : 3 * cols, here] = jnp.where(is_first, 0.0, pltpu.roll(g, 1, 1)).astype(bf16)

    for h in range(gends[1]):
        gcopy[h].wait()

    @pl.when(me >= 0)
    def _():
        prepare(0, gends[1])

    for n in range(len(bounds) - 1):
        lo, hi = bounds[n], bounds[n + 1]
        for h in range(lo, hi):
            acopy[h].wait()
        if n + 2 < len(bounds):
            for h in range(gends[n + 1], gends[n + 2]):
                gcopy[h].wait()

        @pl.when(me >= 0)
        def _(n=n, lo=lo, hi=hi):
            is_end = n + 2 == len(bounds)
            if not is_end:
                prepare(gends[n + 1], gends[n + 2])
            rhs = tile_columns(av, me // 2, (1 + jnp.bitwise_and(me, 1), 2 - jnp.bitwise_and(me, 1)), lo, hi)
            for i in taps:
                here = slice(taps.index(i) * rows, (taps.index(i) + 1) * rows)
                term = tile_terms(gt, rhs, lo, hi, flat, i)
                if n > 0:
                    term = acc[here, :] + term
                if is_end:
                    tile_store(term, i, taps, outs, me, cols)
                else:
                    acc[here, :] = term


def held_kernel(near, taps, me_ref, gt, av, *outs):
    height, batch, width, _ = av.shape
    me = me_ref[0]
    core = jnp.bitwise_and(me, 1)
    rhs = tile_columns(av, me // 2, (1 + core, 2 - core) if near else (3, 0), 0, height)
    for i in taps:
        tile_store(tile_terms(gt, rhs, 0, height, batch * width, i), i, taps, outs, me, gt.shape[0] // 3)


def near_blocks(a, g, me, taps):
    batch, height, width, cin = a.shape
    cols = g.shape[3]
    lanes, flat = cin // 4, batch * width
    block = jax.ShapeDtypeStruct((3 * len(taps) * (lanes // 2), cols), f32)
    res = pl.pallas_call(
        functools.partial(near_kernel, [0, height // 8, height * 3 // 8, height * 11 // 16, height], taps),
        out_shape=[block] * 4 + [pltpu.VMEM((height, batch, width, cin), bf16), pltpu.VMEM((3 * cols, (height + 2) * flat), bf16)],
        in_specs=[SM, HB, HB],
        out_specs=[VM] * 6,
        scratch_shapes=[
            pltpu.VMEM((batch, height, width, cols), bf16),
            pltpu.VMEM((3 * len(taps) * cols, 2 * lanes), f32),
            pltpu.SemaphoreType.DMA((height,)),
            pltpu.SemaphoreType.DMA((height,)),
        ],
        compiler_params=pltpu.CompilerParams(vmem_limit_bytes=NEAR_VMEM),
        cost_estimate=pl.CostEstimate(flops=12 * len(taps) * cols * lanes * height * flat, bytes_accessed=2 * (a.size + g.size), transcendentals=0),
        name="conv_near",
    )(me, g, a)
    return list(res[:4]), res[4], res[5]


def held_blocks(av, gt, me, near, taps):
    height, batch, width, cin = av.shape
    lanes = cin // 4
    cols = gt.shape[0] // 3
    block = jax.ShapeDtypeStruct((3 * len(taps) * (lanes // 2), cols), f32)
    return list(pl.pallas_call(
        functools.partial(held_kernel, near, taps),
        out_shape=[block] * 4,
        in_specs=[SM, VM, VM],
        out_specs=[VM] * 4,
        compiler_params=pltpu.CompilerParams(vmem_limit_bytes=NEXT_VMEM),
        cost_estimate=pl.CostEstimate(flops=12 * len(taps) * cols * lanes * height * batch * width, bytes_accessed=24 * len(taps) * lanes * cols, transcendentals=0),
        name="conv_near_rest" if near else "conv_far",
    )(me, gt, av))


def replica_of(me, flips, k):
    even, odd = flips[k]
    return jnp.bitwise_xor(me, even + jnp.bitwise_and(me, 1) * (odd - even))


def gram_kernel(jobs, pieces, flips, devices, me_ref, *rest):
    parts = len(pieces)
    count = 1 + max(n for piece in pieces for _, _, n in piece)
    arrays, before, (out, rowsums) = rest[:count], rest[count:-2], rest[-2:]
    me = me_ref[0]
    cols = arrays[0].shape[1]
    rowsums[...] = jnp.zeros_like(rowsums)
    size = rowsums.shape[0]
    number = lax.broadcasted_iota(jnp.int32, (size, 128), 0)
    at = jnp.full((size, 128), -1, jnp.int32)
    row = 0
    for lo, hi, pairs in jobs:
        for first in range(0, len(pairs), 16):
            some = pairs[first : first + 16]
            held = {}
            for k in sorted({n for pair in some for n in pair}):
                ((start, _, n),) = [p for p in pieces[k] if p[0] <= lo and hi <= p[1]]
                held[k] = (arrays[n], lo - start)

            def body(i, sums):
                x = {k: ref[pl.ds(pl.multiple_of(i * 8, 8) + skip, 8), :] for k, (ref, skip) in held.items()}
                return [s + x[k] * x[l] for s, (k, l) in zip(sums, some)]

            sums = lax.fori_loop(0, (hi - lo) // 8, body, [jnp.zeros((8, cols), f32) for _ in some], unroll=8)
            for s, (k, l) in zip(sums, some):
                rowsums[row : row + 1, :] = jnp.sum(s, axis=0, keepdims=True)
                a, b = replica_of(me, flips, k), replica_of(me, flips, l)
                at = jnp.where(number == row, jnp.minimum(a, b) * parts + jnp.maximum(a, b), at)
                row += 1
    place = lax.broadcasted_iota(jnp.int32, (size, 128), 1)
    values = jnp.sum(rowsums[...], axis=1, keepdims=True)
    for r in range(out.shape[-2]):
        total = jnp.sum(jnp.where(at == place + r * 128, values, 0.0), axis=0, keepdims=True)
        for part in before:
            total = total + part[r : r + 1, :]
        for n in range(max(devices, 1)):
            if devices:
                out[n, r : r + 1, :] = total
            else:
                out[r : r + 1, :] = total


def gram(jobs, pieces, arrays, before, me, flips, devices):
    parts = len(pieces)
    names = [{n for pair in pairs for n in pair} for _, _, pairs in jobs]
    used = sorted({n for k in range(parts) for lo, hi, n in pieces[k] for (jlo, jhi, _), ks in zip(jobs, names) if k in ks and lo <= jlo and jhi <= hi})
    near = [[(lo, hi, used.index(n)) for lo, hi, n in piece if n in used] for piece in pieces]
    rows = -(-parts * parts // 128)
    shape = (devices, rows, 128) if devices else (rows, 128)
    size = -(-sum(len(pairs) for _, _, pairs in jobs) // 8) * 8
    flat = [arrays[n] for n in used]
    return pl.pallas_call(
        functools.partial(gram_kernel, jobs, near, flips, devices),
        out_shape=jax.ShapeDtypeStruct(shape, f32),
        in_specs=[SM] + [VM] * (len(flat) + len(before)),
        out_specs=VM,
        scratch_shapes=[pltpu.VMEM((size, flat[0].shape[1]), f32)],
        compiler_params=pltpu.CompilerParams(vmem_limit_bytes=NEXT_VMEM),
        cost_estimate=pl.CostEstimate(flops=2 * 128 * sum((hi - lo) * len(pairs) for lo, hi, pairs in jobs), bytes_accessed=sum(4 * x.size for x in flat), transcendentals=0),
        name="gram",
    )(me, *flat, *before)


def mixes_of(sums, parts):
    rows = sums.shape[0]
    place = lax.broadcasted_iota(jnp.int32, (rows, 128), 0) * 128 + lax.broadcasted_iota(jnp.int32, (rows, 128), 1)
    g = {}
    for a in range(parts):
        for b in range(a, parts):
            g[a, b] = g[b, a] = jnp.sum(jnp.where(place == a * parts + b, sums, 0.0), axis=(0, 1), keepdims=True)
    factors = [None] * parts
    count, width = parts, 1
    while count > 1:
        coef = []
        for k in range(count // 2):
            p, qa, qb = g[2 * k, 2 * k + 1], g[2 * k, 2 * k] + 1e-6, g[2 * k + 1, 2 * k + 1] + 1e-6
            coef += [1.0 - p / (2.0 * qa), 1.0 - p / (2.0 * qb)]
        for r in range(parts):
            c = coef[r // width]
            factors[r] = c if factors[r] is None else factors[r] * c
        count, width = count // 2, width * 2
        new = {}
        for k in range(count):
            for l in range(k, count):
                new[k, l] = new[l, k] = sum(coef[x] * coef[y] * g[x, y] for x in (2 * k, 2 * k + 1) for y in (2 * l, 2 * l + 1))
        g = new
    return factors


def final_kernel(pieces, flips, me_ref, sums, weight, momentum, *rest):
    arrays, (new_weight, new_momentum) = rest[:-2], rest[-2:]
    parts = len(pieces)
    me = me_ref[0]
    factors = mixes_of(jnp.sum(sums[...], axis=0), parts)
    mine = []
    for k in range(parts):
        pick, replica = factors[0], replica_of(me, flips, k)
        for r in range(1, parts):
            pick = jnp.where(replica == r, factors[r], pick)
        mine.append(pick)
    step = weight.shape[0] // 9
    for first in range(0, weight.shape[0], step):
        here = slice(first, first + step)
        value = 0.9 * momentum[here, :]
        for k in range(parts):
            ((lo, n),) = [(lo, n) for lo, hi, n in pieces[k] if lo <= first < hi]
            value = value + mine[k] * arrays[n][first - lo : first - lo + step, :]
        new_momentum[here, :] = value
        new_weight[here, :] = weight[here, :] - 0.1 * value


def finish(sums, weight, momentum, pieces, arrays, me, flips):
    depth, cols = weight.shape[0], weight.shape[3]
    w, m = (jnp.transpose(x, (1, 2, 0, 3)).reshape(9 * depth, cols) for x in (weight, momentum))
    outs = pl.pallas_call(
        functools.partial(final_kernel, pieces, flips),
        out_shape=[jax.ShapeDtypeStruct(w.shape, f32)] * 2,
        in_specs=[SM] + [VM] * (3 + len(arrays)),
        out_specs=[VM, VM],
        compiler_params=pltpu.CompilerParams(vmem_limit_bytes=NEXT_VMEM),
        cost_estimate=pl.CostEstimate(flops=2 * w.size * len(pieces), bytes_accessed=4 * w.size * (len(pieces) + 4), transcendentals=0),
        name="final",
    )(me, sums, w, m, *arrays)
    return tuple(jnp.transpose(x.reshape(3, 3, depth, cols), (2, 0, 1, 3)) for x in outs)


def upper_pairs(parts):
    return [(k, l) for k in range(parts) for l in range(k, parts)]


def send(block, parts, flips):
    return lax.ppermute(block, "dp", [(r, r ^ flips[r % 2]) for r in range(parts)])


def by_rows(activations, out_grads, me, parts, devices):
    def exchange(blocks):
        blocks = [b.reshape(-1, b.shape[2]) for b in blocks]
        return blocks[:1] + [send(blocks[k], parts, (k, k)) for k in range(1, parts)]

    middle, av, gt = conv_first(activations, out_grads, me, parts)
    middle = exchange(middle)
    lower = exchange(conv_next(av, gt, me, 1, parts))
    upper = exchange(conv_next(av, gt, me, -1, parts))
    size = middle[0].shape[0]
    pieces = [[(i * size, (i + 1) * size, i * parts + k) for i in range(3)] for k in range(parts)]
    arrays, flips, partial = lower + middle + upper, [(k, k) for k in range(parts)], []
    for i in (1, 0, 2):
        job = (i * size, (i + 1) * size, upper_pairs(parts))
        partial = [gram([job], pieces, arrays, partial, me, flips, devices if i == 2 else 0)]
    return partial[0], pieces, arrays, flips


def by_chips(activations, out_grads, me, parts, devices):
    targets = [(2, 4), (3, 5), (4, 2), (5, 3)]
    near, av, gt = near_blocks(activations, out_grads, me, (0, 1))
    near = [send(block, parts, t) for block, t in zip(near, targets)]
    far = held_blocks(av, gt, me, False, (0, 1, 2))
    own = [far[2], send(far[3], parts, (1, 1))]
    far = [send(far[k], parts, (6 + k, 6 + k)) for k in range(2)]
    rest = held_blocks(av, gt, me, True, (2,))
    rest = [send(block, parts, t) for block, t in zip(rest, targets)]
    flips = [(0, 0), (1, 1), (2, 4), (5, 3), (4, 2), (3, 5), (6, 6), (7, 7)]
    arrays = own + near + far + rest
    split, whole = near[0].shape[0], own[0].shape[0]
    pieces = [[(0, whole, k)] if k < 2 or k > 5 else [(0, split, k), (split, whole, k + 6)] for k in range(parts)]

    def pairs(low, high):
        return [pair for pair in upper_pairs(parts) if low <= pair[1] < high]

    sums = gram([(0, split, pairs(0, 6))], pieces, arrays, [], me, flips, 0)
    sums = gram([(split, whole, pairs(0, 7)), (0, split, pairs(6, 7))], pieces, arrays, [sums], me, flips, 0)
    sums = gram([(0, split, pairs(7, 8)), (split, whole, pairs(7, 8))], pieces, arrays, [sums], me, flips, devices)
    return sums, pieces, arrays, flips


def shards(activations, out_grads, weight, momentum):
    parts = lax.axis_size("dp")
    devices = parts * lax.axis_size("chan")
    me = lax.axis_index("dp").reshape(1).astype(jnp.int32)
    four = parts == 8 and activations.shape[3] % 512 == 0
    sums, pieces, arrays, flips = (by_chips if four else by_rows)(activations, out_grads, me, parts, devices)
    sums = lax.all_to_all(sums, ("dp", "chan"), split_axis=0, concat_axis=0, tiled=True)
    return finish(sums, weight, momentum, pieces, arrays, me, flips)


FIRST_VMEM, NEXT_VMEM, NEAR_VMEM = 30 << 20, 30 << 20, 38 << 20


def solution(mesh):
    in_specs = (
        P("dp", None, None, None),
        P("dp", None, None, "chan"),
        P("dp", None, None, "chan"),
        P("dp", None, None, "chan"),
    )
    out_specs = (P("dp", None, None, "chan"), P("dp", None, None, "chan"))
    return jax.shard_map(shards, mesh=mesh, in_specs=in_specs, out_specs=out_specs, check_vma=False)
```

```python
import functools

import jax
import jax.numpy as jnp
from jax import lax
from jax.experimental import pallas as pl
from jax.experimental.pallas import tpu as pltpu
from jax.sharding import PartitionSpec as P


f32, bf16 = jnp.float32, jnp.bfloat16
SM = pl.BlockSpec(memory_space=pltpu.SMEM)
VM = pl.BlockSpec(memory_space=pltpu.VMEM)
HB = pl.BlockSpec(memory_space=pltpu.HBM)
STEPS = 8


def emit(acc, turned, outs, sem, me, cols):
    rows = turned.shape[1] // len(outs)
    for j in range(3):
        turned[j] = acc[j * cols : (j + 1) * cols, :].T
    copies = []
    for k, out in enumerate(outs):
        first = pl.multiple_of(jnp.bitwise_xor(me, k) * rows, rows)
        copies.append(pltpu.make_async_copy(turned.at[:, pl.ds(first, rows), :], out, sem.at[k]))
    for copy in copies:
        copy.start()
    for copy in copies:
        copy.wait()


def first_kernel(parts, me_ref, g_hbm, a_hbm, *rest):
    outs = rest[:parts]
    av, gt, gv, acc, turned, asem, gsem, osem = rest[parts:]
    height, batch, width, cin = av.shape
    cols = gv.shape[3]
    flat = batch * width
    step = height // STEPS
    acopy = [pltpu.make_async_copy(a_hbm.at[:, h], av.at[h], asem.at[h]) for h in range(height)]
    gcopy = [pltpu.make_async_copy(g_hbm.at[:, i * step : (i + 1) * step], gv.at[:, i * step : (i + 1) * step], gsem.at[i]) for i in range(STEPS)]
    for i in range(STEPS):
        gcopy[i].start()
        for h in range(i * step, (i + 1) * step):
            acopy[h].start()
    gt[:, 0:flat] = jnp.zeros((3 * cols, flat), bf16)
    gt[:, (height + 1) * flat : (height + 2) * flat] = jnp.zeros((3 * cols, flat), bf16)
    column = lax.broadcasted_iota(jnp.int32, (cols, flat), 1) % width
    is_last, is_first = column == width - 1, column == 0

    def prepare(i):
        gcopy[i].wait()
        for h in range(i * step, (i + 1) * step):
            g = gv[:, h].reshape(flat, cols).astype(f32).T
            here = slice((h + 1) * flat, (h + 2) * flat)
            gt[0:cols, here] = jnp.where(is_last, 0.0, pltpu.roll(g, flat - 1, 1)).astype(bf16)
            gt[cols : 2 * cols, here] = g.astype(bf16)
            gt[2 * cols : 3 * cols, here] = jnp.where(is_first, 0.0, pltpu.roll(g, 1, 1)).astype(bf16)

    prepare(0)
    for i in range(STEPS):
        for h in range(i * step, (i + 1) * step):
            acopy[h].wait()
        if i + 1 < STEPS:
            prepare(i + 1)
        rhs = av[i * step : (i + 1) * step].reshape(step * flat, cin)
        term = jnp.dot(gt[:, (i * step + 1) * flat : ((i + 1) * step + 1) * flat], rhs, preferred_element_type=f32)
        acc[...] = term if i == 0 else acc[...] + term
    emit(acc, turned, outs, osem, me_ref[0], cols)


def next_kernel(shift, parts, me_ref, gt, av, *rest):
    outs = rest[:parts]
    acc, turned, osem = rest[parts:]
    height, batch, width, cin = av.shape
    flat = batch * width
    cols = gt.shape[0] // 3
    lhs = gt[:, (1 + shift) * flat : (1 + shift + height) * flat]
    acc[...] = jnp.dot(lhs, av[...].reshape(height * flat, cin), preferred_element_type=f32)
    emit(acc, turned, outs, osem, me_ref[0], cols)


def conv_first(a, g, me, parts):
    batch, height, width, cin = a.shape
    cols = g.shape[3]
    flat = batch * width
    res = pl.pallas_call(
        functools.partial(first_kernel, parts),
        out_shape=[jax.ShapeDtypeStruct((3, cin // parts, cols), f32)] * parts
        + [pltpu.VMEM((height, batch, width, cin), bf16), pltpu.VMEM((3 * cols, (height + 2) * flat), bf16)],
        in_specs=[SM, HB, HB],
        out_specs=[HB] * parts + [VM, VM],
        scratch_shapes=[
            pltpu.VMEM((batch, height, width, cols), bf16),
            pltpu.VMEM((3 * cols, cin), f32),
            pltpu.VMEM((3, cin, cols), f32),
            pltpu.SemaphoreType.DMA((height,)),
            pltpu.SemaphoreType.DMA((STEPS,)),
            pltpu.SemaphoreType.DMA((parts,)),
        ],
        compiler_params=pltpu.CompilerParams(vmem_limit_bytes=FIRST_VMEM),
        cost_estimate=pl.CostEstimate(flops=6 * cols * cin * height * flat, bytes_accessed=2 * (a.size + g.size), transcendentals=0),
        name="conv_first",
    )(me, g, a)
    return list(res[:parts]), res[parts], res[parts + 1]


def conv_next(av, gt, me, shift, parts):
    height, batch, width, cin = av.shape
    cols = gt.shape[0] // 3
    return list(pl.pallas_call(
        functools.partial(next_kernel, shift, parts),
        out_shape=[jax.ShapeDtypeStruct((3, cin // parts, cols), f32)] * parts,
        in_specs=[SM, VM, VM],
        out_specs=[HB] * parts,
        scratch_shapes=[pltpu.VMEM((3 * cols, cin), f32), pltpu.VMEM((3, cin, cols), f32), pltpu.SemaphoreType.DMA((parts,))],
        compiler_params=pltpu.CompilerParams(vmem_limit_bytes=NEXT_VMEM),
        cost_estimate=pl.CostEstimate(flops=6 * cols * cin * height * batch * width, bytes_accessed=12 * cin * cols, transcendentals=0),
        name="conv_next",
    )(me, gt, av))


def tile_terms(gt, rhs, lo, hi, flat, i):
    return jnp.dot(gt[:, (lo + 2 - i) * flat : (hi + 2 - i) * flat], rhs, preferred_element_type=f32)


def tile_columns(av, chip, tiles, lo, hi):
    _, batch, width, cin = av.shape
    lanes = cin // 4
    firsts = [pl.multiple_of(jnp.bitwise_xor(chip, q) * lanes, lanes) for q in tiles]
    return jnp.concatenate([av[lo:hi, :, :, pl.ds(f, lanes)].reshape((hi - lo) * batch * width, lanes) for f in firsts], axis=1)


def tile_store(value, i, taps, outs, me, cols):
    i = taps.index(i)
    is_lower = jnp.bitwise_and(me, 1) == 0
    depth = outs[0].shape[0] // (3 * len(taps))
    for q in range(len(outs) // 2):
        for j in range(3):
            turned = value[j * cols : (j + 1) * cols, q * 2 * depth : (q + 1) * 2 * depth].T
            lower, upper = turned[:depth], turned[depth:]
            here = slice((3 * i + j) * depth, (3 * i + j + 1) * depth)
            outs[2 * q][here, :] = jnp.where(is_lower, lower, upper)
            outs[2 * q + 1][here, :] = jnp.where(is_lower, upper, lower)


def near_kernel(bounds, taps, me_ref, g_hbm, a_hbm, *rest):
    outs = rest[:4]
    av, gt, gv, acc, asem, gsem = rest[4:]
    height, batch, width, _ = av.shape
    cols = gv.shape[3]
    flat = batch * width
    rows = 3 * cols
    me = me_ref[0]
    gends = [0] + [min(b + 1, height) for b in bounds[1:]]
    gcopy = [pltpu.make_async_copy(g_hbm.at[:, h], gv.at[:, h], gsem.at[h]) for h in range(height)]
    acopy = [pltpu.make_async_copy(a_hbm.at[:, h], av.at[h], asem.at[h]) for h in range(height)]
    order = gcopy[: gends[1]]
    for n in range(len(bounds) - 1):
        order += acopy[bounds[n] : bounds[n + 1]]
        if n + 2 < len(bounds):
            order += gcopy[gends[n + 1] : gends[n + 2]]
    for copy in order:
        copy.start()
    gt[:, 0:flat] = jnp.zeros((rows, flat), bf16)
    gt[:, (height + 1) * flat : (height + 2) * flat] = jnp.zeros((rows, flat), bf16)
    column = lax.broadcasted_iota(jnp.int32, (cols, flat), 1) % width
    is_last, is_first = column == width - 1, column == 0

    def prepare(lo, hi):
        for h in range(lo, hi):
            g = gv[:, h].reshape(flat, cols).astype(f32).T
            here = slice((h + 1) * flat, (h + 2) * flat)
            gt[0:cols, here] = jnp.where(is_last, 0.0, pltpu.roll(g, flat - 1, 1)).astype(bf16)
            gt[cols : 2 * cols, here] = g.astype(bf16)
            gt[2 * cols : 3 * cols, here] = jnp.where(is_first, 0.0, pltpu.roll(g, 1, 1)).astype(bf16)

    for h in range(gends[1]):
        gcopy[h].wait()

    @pl.when(me >= 0)
    def _():
        prepare(0, gends[1])

    for n in range(len(bounds) - 1):
        lo, hi = bounds[n], bounds[n + 1]
        for h in range(lo, hi):
            acopy[h].wait()
        if n + 2 < len(bounds):
            for h in range(gends[n + 1], gends[n + 2]):
                gcopy[h].wait()

        @pl.when(me >= 0)
        def _(n=n, lo=lo, hi=hi):
            is_end = n + 2 == len(bounds)
            if not is_end:
                prepare(gends[n + 1], gends[n + 2])
            rhs = tile_columns(av, me // 2, (1 + jnp.bitwise_and(me, 1), 2 - jnp.bitwise_and(me, 1)), lo, hi)
            for i in taps:
                here = slice(taps.index(i) * rows, (taps.index(i) + 1) * rows)
                term = tile_terms(gt, rhs, lo, hi, flat, i)
                if n > 0:
                    term = acc[here, :] + term
                if is_end:
                    tile_store(term, i, taps, outs, me, cols)
                else:
                    acc[here, :] = term


def held_kernel(near, taps, me_ref, gt, av, *outs):
    height, batch, width, _ = av.shape
    me = me_ref[0]
    core = jnp.bitwise_and(me, 1)
    rhs = tile_columns(av, me // 2, (1 + core, 2 - core) if near else (3, 0), 0, height)
    for i in taps:
        tile_store(tile_terms(gt, rhs, 0, height, batch * width, i), i, taps, outs, me, gt.shape[0] // 3)


def near_blocks(a, g, me, taps):
    batch, height, width, cin = a.shape
    cols = g.shape[3]
    lanes, flat = cin // 4, batch * width
    block = jax.ShapeDtypeStruct((3 * len(taps) * (lanes // 2), cols), f32)
    res = pl.pallas_call(
        functools.partial(near_kernel, [height * n // 32 for n in (0, 3, 8, 14, 20, 26, 32)], taps),
        out_shape=[block] * 4 + [pltpu.VMEM((height, batch, width, cin), bf16), pltpu.VMEM((3 * cols, (height + 2) * flat), bf16)],
        in_specs=[SM, HB, HB],
        out_specs=[VM] * 6,
        scratch_shapes=[
            pltpu.VMEM((batch, height, width, cols), bf16),
            pltpu.VMEM((3 * len(taps) * cols, 2 * lanes), f32),
            pltpu.SemaphoreType.DMA((height,)),
            pltpu.SemaphoreType.DMA((height,)),
        ],
        compiler_params=pltpu.CompilerParams(vmem_limit_bytes=NEAR_VMEM),
        cost_estimate=pl.CostEstimate(flops=12 * len(taps) * cols * lanes * height * flat, bytes_accessed=2 * (a.size + g.size), transcendentals=0),
        name="conv_near",
    )(me, g, a)
    return list(res[:4]), res[4], res[5]


def held_blocks(av, gt, me, near, taps):
    height, batch, width, cin = av.shape
    lanes = cin // 4
    cols = gt.shape[0] // 3
    block = jax.ShapeDtypeStruct((3 * len(taps) * (lanes // 2), cols), f32)
    return list(pl.pallas_call(
        functools.partial(held_kernel, near, taps),
        out_shape=[block] * 4,
        in_specs=[SM, VM, VM],
        out_specs=[VM] * 4,
        compiler_params=pltpu.CompilerParams(vmem_limit_bytes=NEXT_VMEM),
        cost_estimate=pl.CostEstimate(flops=12 * len(taps) * cols * lanes * height * batch * width, bytes_accessed=24 * len(taps) * lanes * cols, transcendentals=0),
        name="conv_near_rest" if near else "conv_far",
    )(me, gt, av))


def replica_of(me, flips, k):
    even, odd = flips[k]
    return jnp.bitwise_xor(me, even + jnp.bitwise_and(me, 1) * (odd - even))


def gram_kernel(jobs, pieces, flips, devices, me_ref, *rest):
    parts = len(pieces)
    count = 1 + max(n for piece in pieces for _, _, n in piece)
    arrays, before, (out, rowsums) = rest[:count], rest[count:-2], rest[-2:]
    me = me_ref[0]
    cols = arrays[0].shape[1]
    rowsums[...] = jnp.zeros_like(rowsums)
    size = rowsums.shape[0]
    number = lax.broadcasted_iota(jnp.int32, (size, 128), 0)
    at = jnp.full((size, 128), -1, jnp.int32)
    row = 0
    for lo, hi, pairs in jobs:
        for first in range(0, len(pairs), 16):
            some = pairs[first : first + 16]
            held = {}
            for k in sorted({n for pair in some for n in pair}):
                ((start, _, n),) = [p for p in pieces[k] if p[0] <= lo and hi <= p[1]]
                held[k] = (arrays[n], lo - start)

            def body(i, sums):
                x = {k: ref[pl.ds(pl.multiple_of(i * 8, 8) + skip, 8), :] for k, (ref, skip) in held.items()}
                return [s + x[k] * x[l] for s, (k, l) in zip(sums, some)]

            sums = lax.fori_loop(0, (hi - lo) // 8, body, [jnp.zeros((8, cols), f32) for _ in some], unroll=8)
            for s, (k, l) in zip(sums, some):
                rowsums[row : row + 1, :] = jnp.sum(s, axis=0, keepdims=True)
                a, b = replica_of(me, flips, k), replica_of(me, flips, l)
                at = jnp.where(number == row, jnp.minimum(a, b) * parts + jnp.maximum(a, b), at)
                row += 1
    place = lax.broadcasted_iota(jnp.int32, (size, 128), 1)
    values = jnp.sum(rowsums[...], axis=1, keepdims=True)
    for r in range(out.shape[-2]):
        total = jnp.sum(jnp.where(at == place + r * 128, values, 0.0), axis=0, keepdims=True)
        for part in before:
            total = total + part[r : r + 1, :]
        for n in range(max(devices, 1)):
            if devices:
                out[n, r : r + 1, :] = total
            else:
                out[r : r + 1, :] = total


def gram(jobs, pieces, arrays, before, me, flips, devices):
    parts = len(pieces)
    names = [{n for pair in pairs for n in pair} for _, _, pairs in jobs]
    used = sorted({n for k in range(parts) for lo, hi, n in pieces[k] for (jlo, jhi, _), ks in zip(jobs, names) if k in ks and lo <= jlo and jhi <= hi})
    near = [[(lo, hi, used.index(n)) for lo, hi, n in piece if n in used] for piece in pieces]
    rows = -(-parts * parts // 128)
    shape = (devices, rows, 128) if devices else (rows, 128)
    size = -(-sum(len(pairs) for _, _, pairs in jobs) // 8) * 8
    flat = [arrays[n] for n in used]
    return pl.pallas_call(
        functools.partial(gram_kernel, jobs, near, flips, devices),
        out_shape=jax.ShapeDtypeStruct(shape, f32),
        in_specs=[SM] + [VM] * (len(flat) + len(before)),
        out_specs=VM,
        scratch_shapes=[pltpu.VMEM((size, flat[0].shape[1]), f32)],
        compiler_params=pltpu.CompilerParams(vmem_limit_bytes=NEXT_VMEM),
        cost_estimate=pl.CostEstimate(flops=2 * 128 * sum((hi - lo) * len(pairs) for lo, hi, pairs in jobs), bytes_accessed=sum(4 * x.size for x in flat), transcendentals=0),
        name="gram",
    )(me, *flat, *before)


def mixes_of(sums, parts):
    rows = sums.shape[0]
    place = lax.broadcasted_iota(jnp.int32, (rows, 128), 0) * 128 + lax.broadcasted_iota(jnp.int32, (rows, 128), 1)
    g = {}
    for a in range(parts):
        for b in range(a, parts):
            g[a, b] = g[b, a] = jnp.sum(jnp.where(place == a * parts + b, sums, 0.0), axis=(0, 1), keepdims=True)
    factors = [None] * parts
    count, width = parts, 1
    while count > 1:
        coef = []
        for k in range(count // 2):
            p, qa, qb = g[2 * k, 2 * k + 1], g[2 * k, 2 * k] + 1e-6, g[2 * k + 1, 2 * k + 1] + 1e-6
            coef += [1.0 - p / (2.0 * qa), 1.0 - p / (2.0 * qb)]
        for r in range(parts):
            c = coef[r // width]
            factors[r] = c if factors[r] is None else factors[r] * c
        count, width = count // 2, width * 2
        new = {}
        for k in range(count):
            for l in range(k, count):
                new[k, l] = new[l, k] = sum(coef[x] * coef[y] * g[x, y] for x in (2 * k, 2 * k + 1) for y in (2 * l, 2 * l + 1))
        g = new
    return factors


def final_kernel(pieces, flips, me_ref, sums, weight, momentum, *rest):
    arrays, (new_weight, new_momentum) = rest[:-2], rest[-2:]
    parts = len(pieces)
    me = me_ref[0]
    factors = mixes_of(jnp.sum(sums[...], axis=0), parts)
    mine = []
    for k in range(parts):
        pick, replica = factors[0], replica_of(me, flips, k)
        for r in range(1, parts):
            pick = jnp.where(replica == r, factors[r], pick)
        mine.append(pick)
    step = weight.shape[0] // 9
    for first in range(0, weight.shape[0], step):
        here = slice(first, first + step)
        value = 0.9 * momentum[here, :]
        for k in range(parts):
            ((lo, n),) = [(lo, n) for lo, hi, n in pieces[k] if lo <= first < hi]
            value = value + mine[k] * arrays[n][first - lo : first - lo + step, :]
        new_momentum[here, :] = value
        new_weight[here, :] = weight[here, :] - 0.1 * value


def finish(sums, weight, momentum, pieces, arrays, me, flips):
    depth, cols = weight.shape[0], weight.shape[3]
    w, m = (jnp.transpose(x, (1, 2, 0, 3)).reshape(9 * depth, cols) for x in (weight, momentum))
    outs = pl.pallas_call(
        functools.partial(final_kernel, pieces, flips),
        out_shape=[jax.ShapeDtypeStruct(w.shape, f32)] * 2,
        in_specs=[SM] + [VM] * (3 + len(arrays)),
        out_specs=[VM, VM],
        compiler_params=pltpu.CompilerParams(vmem_limit_bytes=NEXT_VMEM),
        cost_estimate=pl.CostEstimate(flops=2 * w.size * len(pieces), bytes_accessed=4 * w.size * (len(pieces) + 4), transcendentals=0),
        name="final",
    )(me, sums, w, m, *arrays)
    return tuple(jnp.transpose(x.reshape(3, 3, depth, cols), (2, 0, 1, 3)) for x in outs)


def upper_pairs(parts):
    return [(k, l) for k in range(parts) for l in range(k, parts)]


def send(block, parts, flips):
    return lax.ppermute(block, "dp", [(r, r ^ flips[r % 2]) for r in range(parts)])


def by_rows(activations, out_grads, me, parts, devices):
    def exchange(blocks):
        blocks = [b.reshape(-1, b.shape[2]) for b in blocks]
        return blocks[:1] + [send(blocks[k], parts, (k, k)) for k in range(1, parts)]

    middle, av, gt = conv_first(activations, out_grads, me, parts)
    middle = exchange(middle)
    lower = exchange(conv_next(av, gt, me, 1, parts))
    upper = exchange(conv_next(av, gt, me, -1, parts))
    size = middle[0].shape[0]
    pieces = [[(i * size, (i + 1) * size, i * parts + k) for i in range(3)] for k in range(parts)]
    arrays, flips, partial = lower + middle + upper, [(k, k) for k in range(parts)], []
    for i in (1, 0, 2):
        job = (i * size, (i + 1) * size, upper_pairs(parts))
        partial = [gram([job], pieces, arrays, partial, me, flips, devices if i == 2 else 0)]
    return partial[0], pieces, arrays, flips


def by_chips(activations, out_grads, me, parts, devices):
    targets = [(2, 4), (3, 5), (4, 2), (5, 3)]

    def near_out(blocks):
        return [send(block, parts, t) for block, t in zip(blocks, targets)]

    def far_out(blocks):
        far = [send(blocks[k], parts, (6 + k, 6 + k)) for k in range(2)]
        return [blocks[2], send(blocks[3], parts, (1, 1))], far

    near, av, gt = near_blocks(activations, out_grads, me, (0, 1))
    near = near_out(near)
    far = held_blocks(av, gt, me, False, (0, 1))
    own, far = far_out(far)
    rest = held_blocks(av, gt, me, True, (2,))
    rest = near_out(rest)
    tail = held_blocks(av, gt, me, False, (2,))
    tail_own, tail = far_out(tail)
    flips = [(0, 0), (1, 1), (2, 4), (5, 3), (4, 2), (3, 5), (6, 6), (7, 7)]
    arrays = own + near + far + tail_own + rest + tail
    split = near[0].shape[0]
    whole = split + rest[0].shape[0]
    pieces = [[(0, split, k), (split, whole, parts + k)] for k in range(parts)]

    def pairs(low, high):
        return [pair for pair in upper_pairs(parts) if low <= pair[1] < high]

    sums = gram([(0, split, pairs(0, 6))], pieces, arrays, [], me, flips, 0)
    sums = gram([(0, split, pairs(6, 8))], pieces, arrays, [sums], me, flips, 0)
    sums = gram([(split, whole, pairs(0, 8))], pieces, arrays, [sums], me, flips, devices)
    return sums, pieces, arrays, flips


def shards(activations, out_grads, weight, momentum):
    parts = lax.axis_size("dp")
    devices = parts * lax.axis_size("chan")
    me = lax.axis_index("dp").reshape(1).astype(jnp.int32)
    four = parts == 8 and activations.shape[3] % 512 == 0
    sums, pieces, arrays, flips = (by_chips if four else by_rows)(activations, out_grads, me, parts, devices)
    sums = lax.all_to_all(sums, ("dp", "chan"), split_axis=0, concat_axis=0, tiled=True)
    return finish(sums, weight, momentum, pieces, arrays, me, flips)


FIRST_VMEM, NEXT_VMEM, NEAR_VMEM = 30 << 20, 30 << 20, 38 << 20


def solution(mesh):
    in_specs = (
        P("dp", None, None, None),
        P("dp", None, None, "chan"),
        P("dp", None, None, "chan"),
        P("dp", None, None, "chan"),
    )
    out_specs = (P("dp", None, None, "chan"), P("dp", None, None, "chan"))
    return jax.shard_map(shards, mesh=mesh, in_specs=in_specs, out_specs=out_specs, check_vma=False)
```

```python
import functools

import jax
import jax.numpy as jnp
from jax import lax
from jax.experimental import pallas as pl
from jax.experimental.pallas import tpu as pltpu
from jax.sharding import PartitionSpec as P


f32, bf16 = jnp.float32, jnp.bfloat16
SM = pl.BlockSpec(memory_space=pltpu.SMEM)
VM = pl.BlockSpec(memory_space=pltpu.VMEM)
HB = pl.BlockSpec(memory_space=pltpu.HBM)
STEPS = 8


def emit(acc, turned, outs, sem, me, cols):
    rows = turned.shape[1] // len(outs)
    for j in range(3):
        turned[j] = acc[j * cols : (j + 1) * cols, :].T
    copies = []
    for k, out in enumerate(outs):
        first = pl.multiple_of(jnp.bitwise_xor(me, k) * rows, rows)
        copies.append(pltpu.make_async_copy(turned.at[:, pl.ds(first, rows), :], out, sem.at[k]))
    for copy in copies:
        copy.start()
    for copy in copies:
        copy.wait()


def first_kernel(parts, me_ref, g_hbm, a_hbm, *rest):
    outs = rest[:parts]
    av, gt, gv, acc, turned, asem, gsem, osem = rest[parts:]
    height, batch, width, cin = av.shape
    cols = gv.shape[3]
    flat = batch * width
    step = height // STEPS
    acopy = [pltpu.make_async_copy(a_hbm.at[:, h], av.at[h], asem.at[h]) for h in range(height)]
    gcopy = [pltpu.make_async_copy(g_hbm.at[:, i * step : (i + 1) * step], gv.at[:, i * step : (i + 1) * step], gsem.at[i]) for i in range(STEPS)]
    for i in range(STEPS):
        gcopy[i].start()
        for h in range(i * step, (i + 1) * step):
            acopy[h].start()
    gt[:, 0:flat] = jnp.zeros((3 * cols, flat), bf16)
    gt[:, (height + 1) * flat : (height + 2) * flat] = jnp.zeros((3 * cols, flat), bf16)
    column = lax.broadcasted_iota(jnp.int32, (cols, flat), 1) % width
    is_last, is_first = column == width - 1, column == 0

    def prepare(i):
        gcopy[i].wait()
        for h in range(i * step, (i + 1) * step):
            g = gv[:, h].reshape(flat, cols).astype(f32).T
            here = slice((h + 1) * flat, (h + 2) * flat)
            gt[0:cols, here] = jnp.where(is_last, 0.0, pltpu.roll(g, flat - 1, 1)).astype(bf16)
            gt[cols : 2 * cols, here] = g.astype(bf16)
            gt[2 * cols : 3 * cols, here] = jnp.where(is_first, 0.0, pltpu.roll(g, 1, 1)).astype(bf16)

    prepare(0)
    for i in range(STEPS):
        for h in range(i * step, (i + 1) * step):
            acopy[h].wait()
        if i + 1 < STEPS:
            prepare(i + 1)
        rhs = av[i * step : (i + 1) * step].reshape(step * flat, cin)
        term = jnp.dot(gt[:, (i * step + 1) * flat : ((i + 1) * step + 1) * flat], rhs, preferred_element_type=f32)
        acc[...] = term if i == 0 else acc[...] + term
    emit(acc, turned, outs, osem, me_ref[0], cols)


def next_kernel(shift, parts, me_ref, gt, av, *rest):
    outs = rest[:parts]
    acc, turned, osem = rest[parts:]
    height, batch, width, cin = av.shape
    flat = batch * width
    cols = gt.shape[0] // 3
    lhs = gt[:, (1 + shift) * flat : (1 + shift + height) * flat]
    acc[...] = jnp.dot(lhs, av[...].reshape(height * flat, cin), preferred_element_type=f32)
    emit(acc, turned, outs, osem, me_ref[0], cols)


def conv_first(a, g, me, parts):
    batch, height, width, cin = a.shape
    cols = g.shape[3]
    flat = batch * width
    res = pl.pallas_call(
        functools.partial(first_kernel, parts),
        out_shape=[jax.ShapeDtypeStruct((3, cin // parts, cols), f32)] * parts
        + [pltpu.VMEM((height, batch, width, cin), bf16), pltpu.VMEM((3 * cols, (height + 2) * flat), bf16)],
        in_specs=[SM, HB, HB],
        out_specs=[HB] * parts + [VM, VM],
        scratch_shapes=[
            pltpu.VMEM((batch, height, width, cols), bf16),
            pltpu.VMEM((3 * cols, cin), f32),
            pltpu.VMEM((3, cin, cols), f32),
            pltpu.SemaphoreType.DMA((height,)),
            pltpu.SemaphoreType.DMA((STEPS,)),
            pltpu.SemaphoreType.DMA((parts,)),
        ],
        compiler_params=pltpu.CompilerParams(vmem_limit_bytes=FIRST_VMEM),
        cost_estimate=pl.CostEstimate(flops=6 * cols * cin * height * flat, bytes_accessed=2 * (a.size + g.size), transcendentals=0),
        name="conv_first",
    )(me, g, a)
    return list(res[:parts]), res[parts], res[parts + 1]


def conv_next(av, gt, me, shift, parts):
    height, batch, width, cin = av.shape
    cols = gt.shape[0] // 3
    return list(pl.pallas_call(
        functools.partial(next_kernel, shift, parts),
        out_shape=[jax.ShapeDtypeStruct((3, cin // parts, cols), f32)] * parts,
        in_specs=[SM, VM, VM],
        out_specs=[HB] * parts,
        scratch_shapes=[pltpu.VMEM((3 * cols, cin), f32), pltpu.VMEM((3, cin, cols), f32), pltpu.SemaphoreType.DMA((parts,))],
        compiler_params=pltpu.CompilerParams(vmem_limit_bytes=NEXT_VMEM),
        cost_estimate=pl.CostEstimate(flops=6 * cols * cin * height * batch * width, bytes_accessed=12 * cin * cols, transcendentals=0),
        name="conv_next",
    )(me, gt, av))


def tile_terms(gt, rhs, lo, hi, flat, i):
    return jnp.dot(gt[:, (lo + 2 - i) * flat : (hi + 2 - i) * flat], rhs, preferred_element_type=f32)


def tile_columns(av, chip, tiles, lo, hi):
    _, batch, width, cin = av.shape
    lanes = cin // 4
    firsts = [pl.multiple_of(jnp.bitwise_xor(chip, q) * lanes, lanes) for q in tiles]
    return jnp.concatenate([av[lo:hi, :, :, pl.ds(f, lanes)].reshape((hi - lo) * batch * width, lanes) for f in firsts], axis=1)


def tile_store(value, i, taps, outs, me, cols):
    i = taps.index(i)
    is_lower = jnp.bitwise_and(me, 1) == 0
    depth = outs[0].shape[0] // (3 * len(taps))
    for q in range(len(outs) // 2):
        for j in range(3):
            turned = value[j * cols : (j + 1) * cols, q * 2 * depth : (q + 1) * 2 * depth].T
            lower, upper = turned[:depth], turned[depth:]
            here = slice((3 * i + j) * depth, (3 * i + j + 1) * depth)
            outs[2 * q][here, :] = jnp.where(is_lower, lower, upper)
            outs[2 * q + 1][here, :] = jnp.where(is_lower, upper, lower)


def near_kernel(bounds, taps, me_ref, g_hbm, a_hbm, *rest):
    outs = rest[:4]
    av, gt, gv, acc, asem, gsem = rest[4:]
    height, batch, width, _ = av.shape
    cols = gv.shape[3]
    flat = batch * width
    rows = 3 * cols
    me = me_ref[0]
    gends = [0] + [min(b + 1, height) for b in bounds[1:]]
    gcopy = [pltpu.make_async_copy(g_hbm.at[:, h], gv.at[:, h], gsem.at[h]) for h in range(height)]
    acopy = [pltpu.make_async_copy(a_hbm.at[:, h], av.at[h], asem.at[h]) for h in range(height)]
    order = gcopy[: gends[1]]
    for n in range(len(bounds) - 1):
        order += acopy[bounds[n] : bounds[n + 1]]
        if n + 2 < len(bounds):
            order += gcopy[gends[n + 1] : gends[n + 2]]
    for copy in order:
        copy.start()
    gt[:, 0:flat] = jnp.zeros((rows, flat), bf16)
    gt[:, (height + 1) * flat : (height + 2) * flat] = jnp.zeros((rows, flat), bf16)
    column = lax.broadcasted_iota(jnp.int32, (cols, flat), 1) % width
    is_last, is_first = column == width - 1, column == 0

    def prepare(lo, hi):
        for h in range(lo, hi):
            g = gv[:, h].reshape(flat, cols).T
            here = slice((h + 1) * flat, (h + 2) * flat)
            gt[0:cols, here] = jnp.where(is_last, jnp.zeros_like(g), pltpu.roll(g, flat - 1, 1))
            gt[cols : 2 * cols, here] = g
            gt[2 * cols : 3 * cols, here] = jnp.where(is_first, jnp.zeros_like(g), pltpu.roll(g, 1, 1))

    for h in range(gends[1]):
        gcopy[h].wait()

    @pl.when(me >= 0)
    def _():
        prepare(0, gends[1])

    for n in range(len(bounds) - 1):
        lo, hi = bounds[n], bounds[n + 1]
        for h in range(lo, hi):
            acopy[h].wait()
        if n + 2 < len(bounds):
            for h in range(gends[n + 1], gends[n + 2]):
                gcopy[h].wait()

        @pl.when(me >= 0)
        def _(n=n, lo=lo, hi=hi):
            is_end = n + 2 == len(bounds)
            if not is_end:
                prepare(gends[n + 1], gends[n + 2])
            rhs = tile_columns(av, me // 2, (1 + jnp.bitwise_and(me, 1), 2 - jnp.bitwise_and(me, 1)), lo, hi)
            for i in taps:
                here = slice(taps.index(i) * rows, (taps.index(i) + 1) * rows)
                term = tile_terms(gt, rhs, lo, hi, flat, i)
                if n > 0:
                    term = acc[here, :] + term
                if is_end:
                    tile_store(term, i, taps, outs, me, cols)
                else:
                    acc[here, :] = term


def held_kernel(near, taps, me_ref, gt, av, *outs):
    height, batch, width, _ = av.shape
    me = me_ref[0]
    core = jnp.bitwise_and(me, 1)
    rhs = tile_columns(av, me // 2, (1 + core, 2 - core) if near else (3, 0), 0, height)
    for i in taps:
        tile_store(tile_terms(gt, rhs, 0, height, batch * width, i), i, taps, outs, me, gt.shape[0] // 3)


def near_blocks(a, g, me, taps):
    batch, height, width, cin = a.shape
    cols = g.shape[3]
    lanes, flat = cin // 4, batch * width
    block = jax.ShapeDtypeStruct((3 * len(taps) * (lanes // 2), cols), f32)
    res = pl.pallas_call(
        functools.partial(near_kernel, [height * n // 32 for n in (0, 3, 8, 14, 20, 26, 32)], taps),
        out_shape=[block] * 4 + [pltpu.VMEM((height, batch, width, cin), bf16), pltpu.VMEM((3 * cols, (height + 2) * flat), bf16)],
        in_specs=[SM, HB, HB],
        out_specs=[VM] * 6,
        scratch_shapes=[
            pltpu.VMEM((batch, height, width, cols), bf16),
            pltpu.VMEM((3 * len(taps) * cols, 2 * lanes), f32),
            pltpu.SemaphoreType.DMA((height,)),
            pltpu.SemaphoreType.DMA((height,)),
        ],
        compiler_params=pltpu.CompilerParams(vmem_limit_bytes=NEAR_VMEM),
        cost_estimate=pl.CostEstimate(flops=12 * len(taps) * cols * lanes * height * flat, bytes_accessed=2 * (a.size + g.size), transcendentals=0),
        name="conv_near",
    )(me, g, a)
    return list(res[:4]), res[4], res[5]


def held_blocks(av, gt, me, near, taps):
    height, batch, width, cin = av.shape
    lanes = cin // 4
    cols = gt.shape[0] // 3
    block = jax.ShapeDtypeStruct((3 * len(taps) * (lanes // 2), cols), f32)
    return list(pl.pallas_call(
        functools.partial(held_kernel, near, taps),
        out_shape=[block] * 4,
        in_specs=[SM, VM, VM],
        out_specs=[VM] * 4,
        compiler_params=pltpu.CompilerParams(vmem_limit_bytes=NEXT_VMEM),
        cost_estimate=pl.CostEstimate(flops=12 * len(taps) * cols * lanes * height * batch * width, bytes_accessed=24 * len(taps) * lanes * cols, transcendentals=0),
        name="conv_near_rest" if near else "conv_far",
    )(me, gt, av))


def replica_of(me, flips, k):
    even, odd = flips[k]
    return jnp.bitwise_xor(me, even + jnp.bitwise_and(me, 1) * (odd - even))


def gram_kernel(jobs, pieces, flips, devices, me_ref, *rest):
    parts = len(pieces)
    count = 1 + max(n for piece in pieces for _, _, n in piece)
    arrays, before, (out, rowsums) = rest[:count], rest[count:-2], rest[-2:]
    me = me_ref[0]
    cols = arrays[0].shape[1]
    rowsums[...] = jnp.zeros_like(rowsums)
    size = rowsums.shape[0]
    number = lax.broadcasted_iota(jnp.int32, (size, 128), 0)
    at = jnp.full((size, 128), -1, jnp.int32)
    row = 0
    for lo, hi, pairs in jobs:
        for first in range(0, len(pairs), 16):
            some = pairs[first : first + 16]
            held = {}
            for k in sorted({n for pair in some for n in pair}):
                ((start, _, n),) = [p for p in pieces[k] if p[0] <= lo and hi <= p[1]]
                held[k] = (arrays[n], lo - start)

            def body(i, sums):
                x = {k: ref[pl.ds(pl.multiple_of(i * 8, 8) + skip, 8), :] for k, (ref, skip) in held.items()}
                return [s + x[k] * x[l] for s, (k, l) in zip(sums, some)]

            sums = lax.fori_loop(0, (hi - lo) // 8, body, [jnp.zeros((8, cols), f32) for _ in some], unroll=8)
            for s, (k, l) in zip(sums, some):
                rowsums[row : row + 1, :] = jnp.sum(s, axis=0, keepdims=True)
                a, b = replica_of(me, flips, k), replica_of(me, flips, l)
                at = jnp.where(number == row, jnp.minimum(a, b) * parts + jnp.maximum(a, b), at)
                row += 1
    place = lax.broadcasted_iota(jnp.int32, (size, 128), 1)
    values = jnp.sum(rowsums[...], axis=1, keepdims=True)
    for r in range(out.shape[-2]):
        total = jnp.sum(jnp.where(at == place + r * 128, values, 0.0), axis=0, keepdims=True)
        for part in before:
            total = total + part[r : r + 1, :]
        for n in range(max(devices, 1)):
            if devices:
                out[n, r : r + 1, :] = total
            else:
                out[r : r + 1, :] = total


def gram(jobs, pieces, arrays, before, me, flips, devices):
    parts = len(pieces)
    names = [{n for pair in pairs for n in pair} for _, _, pairs in jobs]
    used = sorted({n for k in range(parts) for lo, hi, n in pieces[k] for (jlo, jhi, _), ks in zip(jobs, names) if k in ks and lo <= jlo and jhi <= hi})
    near = [[(lo, hi, used.index(n)) for lo, hi, n in piece if n in used] for piece in pieces]
    rows = -(-parts * parts // 128)
    shape = (devices, rows, 128) if devices else (rows, 128)
    size = -(-sum(len(pairs) for _, _, pairs in jobs) // 8) * 8
    flat = [arrays[n] for n in used]
    return pl.pallas_call(
        functools.partial(gram_kernel, jobs, near, flips, devices),
        out_shape=jax.ShapeDtypeStruct(shape, f32),
        in_specs=[SM] + [VM] * (len(flat) + len(before)),
        out_specs=VM,
        scratch_shapes=[pltpu.VMEM((size, flat[0].shape[1]), f32)],
        compiler_params=pltpu.CompilerParams(vmem_limit_bytes=NEXT_VMEM),
        cost_estimate=pl.CostEstimate(flops=2 * 128 * sum((hi - lo) * len(pairs) for lo, hi, pairs in jobs), bytes_accessed=sum(4 * x.size for x in flat), transcendentals=0),
        name="gram",
    )(me, *flat, *before)


def mixes_of(sums, parts):
    rows = sums.shape[0]
    place = lax.broadcasted_iota(jnp.int32, (rows, 128), 0) * 128 + lax.broadcasted_iota(jnp.int32, (rows, 128), 1)
    g = {}
    for a in range(parts):
        for b in range(a, parts):
            g[a, b] = g[b, a] = jnp.sum(jnp.where(place == a * parts + b, sums, 0.0), axis=(0, 1), keepdims=True)
    factors = [None] * parts
    count, width = parts, 1
    while count > 1:
        coef = []
        for k in range(count // 2):
            p, qa, qb = g[2 * k, 2 * k + 1], g[2 * k, 2 * k] + 1e-6, g[2 * k + 1, 2 * k + 1] + 1e-6
            coef += [1.0 - p / (2.0 * qa), 1.0 - p / (2.0 * qb)]
        for r in range(parts):
            c = coef[r // width]
            factors[r] = c if factors[r] is None else factors[r] * c
        count, width = count // 2, width * 2
        new = {}
        for k in range(count):
            for l in range(k, count):
                new[k, l] = new[l, k] = sum(coef[x] * coef[y] * g[x, y] for x in (2 * k, 2 * k + 1) for y in (2 * l, 2 * l + 1))
        g = new
    return factors


def final_kernel(pieces, flips, me_ref, sums, weight, momentum, *rest):
    arrays, (weight_out, momentum_out, new_weight, new_momentum, sem) = rest[:-5], rest[-5:]
    parts = len(pieces)
    copies = []
    me = me_ref[0]
    factors = mixes_of(jnp.sum(sums[...], axis=0), parts)
    mine = []
    for k in range(parts):
        pick, replica = factors[0], replica_of(me, flips, k)
        for r in range(1, parts):
            pick = jnp.where(replica == r, factors[r], pick)
        mine.append(pick)
    step = weight.shape[0] // 9
    for first in range(0, weight.shape[0], step):
        here = slice(first, first + step)
        value = 0.9 * momentum[here, :]
        for k in range(parts):
            ((lo, n),) = [(lo, n) for lo, hi, n in pieces[k] if lo <= first < hi]
            value = value + mine[k] * arrays[n][first - lo : first - lo + step, :]
        new_momentum[here, :] = value
        new_weight[here, :] = weight[here, :] - 0.1 * value
        if (first // step) % 3 == 2:
            third = slice(first - 2 * step, first + step)
            for held, out in ((new_weight, weight_out), (new_momentum, momentum_out)):
                copies.append(pltpu.make_async_copy(held.at[third], out.at[third], sem.at[len(copies)]))
                copies[-1].start()
    for copy in copies:
        copy.wait()


def finish(sums, weight, momentum, pieces, arrays, me, flips):
    depth, cols = weight.shape[0], weight.shape[3]
    w, m = (jnp.transpose(x, (1, 2, 0, 3)).reshape(9 * depth, cols) for x in (weight, momentum))
    outs = pl.pallas_call(
        functools.partial(final_kernel, pieces, flips),
        out_shape=[jax.ShapeDtypeStruct(w.shape, f32)] * 2,
        in_specs=[SM] + [VM] * (3 + len(arrays)),
        out_specs=[HB, HB],
        scratch_shapes=[pltpu.VMEM(w.shape, f32), pltpu.VMEM(w.shape, f32), pltpu.SemaphoreType.DMA((6,))],
        compiler_params=pltpu.CompilerParams(vmem_limit_bytes=NEXT_VMEM),
        cost_estimate=pl.CostEstimate(flops=2 * w.size * len(pieces), bytes_accessed=4 * w.size * (len(pieces) + 4), transcendentals=0),
        name="final",
    )(me, sums, w, m, *arrays)
    return tuple(jnp.transpose(x.reshape(3, 3, depth, cols), (2, 0, 1, 3)) for x in outs)


def upper_pairs(parts):
    return [(k, l) for k in range(parts) for l in range(k, parts)]


def send(block, parts, flips):
    return lax.ppermute(block, "dp", [(r, r ^ flips[r % 2]) for r in range(parts)])


def by_rows(activations, out_grads, me, parts, devices):
    def exchange(blocks):
        blocks = [b.reshape(-1, b.shape[2]) for b in blocks]
        return blocks[:1] + [send(blocks[k], parts, (k, k)) for k in range(1, parts)]

    middle, av, gt = conv_first(activations, out_grads, me, parts)
    middle = exchange(middle)
    lower = exchange(conv_next(av, gt, me, 1, parts))
    upper = exchange(conv_next(av, gt, me, -1, parts))
    size = middle[0].shape[0]
    pieces = [[(i * size, (i + 1) * size, i * parts + k) for i in range(3)] for k in range(parts)]
    arrays, flips, partial = lower + middle + upper, [(k, k) for k in range(parts)], []
    for i in (1, 0, 2):
        job = (i * size, (i + 1) * size, upper_pairs(parts))
        partial = [gram([job], pieces, arrays, partial, me, flips, devices if i == 2 else 0)]
    return partial[0], pieces, arrays, flips


def by_chips(activations, out_grads, me, parts, devices):
    targets = [(2, 4), (3, 5), (4, 2), (5, 3)]

    def near_out(blocks):
        return [send(block, parts, t) for block, t in zip(blocks, targets)]

    def far_out(blocks):
        far = [send(blocks[k], parts, (6 + k, 6 + k)) for k in range(2)]
        return [blocks[2], send(blocks[3], parts, (1, 1))], far

    near, av, gt = near_blocks(activations, out_grads, me, (0, 1))
    near = near_out(near)
    far = held_blocks(av, gt, me, False, (0, 1))
    own, far = far_out(far)
    rest = held_blocks(av, gt, me, True, (2,))
    rest = near_out(rest)
    tail = held_blocks(av, gt, me, False, (2,))
    tail_own, tail = far_out(tail)
    flips = [(0, 0), (1, 1), (2, 4), (5, 3), (4, 2), (3, 5), (6, 6), (7, 7)]
    arrays = own + near + far + tail_own + rest + tail
    split = near[0].shape[0]
    whole = split + rest[0].shape[0]
    pieces = [[(0, split, k), (split, whole, parts + k)] for k in range(parts)]

    def pairs(low, high):
        return [pair for pair in upper_pairs(parts) if low <= pair[1] < high]

    sums = gram([(0, split, pairs(0, 6))], pieces, arrays, [], me, flips, 0)
    sums = gram([(0, split, pairs(6, 8))], pieces, arrays, [sums], me, flips, 0)
    sums = gram([(split, whole, pairs(0, 7))], pieces, arrays, [sums], me, flips, 0)
    sums = gram([(split, whole, pairs(7, 8))], pieces, arrays, [sums], me, flips, devices)
    return sums, pieces, arrays, flips


def shards(activations, out_grads, weight, momentum):
    parts = lax.axis_size("dp")
    devices = parts * lax.axis_size("chan")
    me = lax.axis_index("dp").reshape(1).astype(jnp.int32)
    four = parts == 8 and activations.shape[3] % 512 == 0
    sums, pieces, arrays, flips = (by_chips if four else by_rows)(activations, out_grads, me, parts, devices)
    sums = lax.all_to_all(sums, ("dp", "chan"), split_axis=0, concat_axis=0, tiled=True)
    return finish(sums, weight, momentum, pieces, arrays, me, flips)


FIRST_VMEM, NEXT_VMEM, NEAR_VMEM = 30 << 20, 30 << 20, 38 << 20


def solution(mesh):
    in_specs = (
        P("dp", None, None, None),
        P("dp", None, None, "chan"),
        P("dp", None, None, "chan"),
        P("dp", None, None, "chan"),
    )
    out_specs = (P("dp", None, None, "chan"), P("dp", None, None, "chan"))
    return jax.shard_map(shards, mesh=mesh, in_specs=in_specs, out_specs=out_specs, check_vma=False)
```

```python
import functools

import jax
import jax.numpy as jnp
from jax import lax
from jax.experimental import pallas as pl
from jax.experimental.pallas import tpu as pltpu
from jax.sharding import PartitionSpec as P


f32, bf16 = jnp.float32, jnp.bfloat16
SM = pl.BlockSpec(memory_space=pltpu.SMEM)
VM = pl.BlockSpec(memory_space=pltpu.VMEM)
HB = pl.BlockSpec(memory_space=pltpu.HBM)
STEPS = 8


def emit(acc, turned, outs, sem, me, cols):
    rows = turned.shape[1] // len(outs)
    for j in range(3):
        turned[j] = acc[j * cols : (j + 1) * cols, :].T
    copies = []
    for k, out in enumerate(outs):
        first = pl.multiple_of(jnp.bitwise_xor(me, k) * rows, rows)
        copies.append(pltpu.make_async_copy(turned.at[:, pl.ds(first, rows), :], out, sem.at[k]))
    for copy in copies:
        copy.start()
    for copy in copies:
        copy.wait()


def first_kernel(parts, me_ref, g_hbm, a_hbm, *rest):
    outs = rest[:parts]
    av, gt, gv, acc, turned, asem, gsem, osem = rest[parts:]
    height, batch, width, cin = av.shape
    cols = gv.shape[3]
    flat = batch * width
    step = height // STEPS
    acopy = [pltpu.make_async_copy(a_hbm.at[:, h], av.at[h], asem.at[h]) for h in range(height)]
    gcopy = [pltpu.make_async_copy(g_hbm.at[:, i * step : (i + 1) * step], gv.at[:, i * step : (i + 1) * step], gsem.at[i]) for i in range(STEPS)]
    for i in range(STEPS):
        gcopy[i].start()
        for h in range(i * step, (i + 1) * step):
            acopy[h].start()
    gt[:, 0:flat] = jnp.zeros((3 * cols, flat), bf16)
    gt[:, (height + 1) * flat : (height + 2) * flat] = jnp.zeros((3 * cols, flat), bf16)
    column = lax.broadcasted_iota(jnp.int32, (cols, flat), 1) % width
    is_last, is_first = column == width - 1, column == 0

    def prepare(i):
        gcopy[i].wait()
        for h in range(i * step, (i + 1) * step):
            g = gv[:, h].reshape(flat, cols).astype(f32).T
            here = slice((h + 1) * flat, (h + 2) * flat)
            gt[0:cols, here] = jnp.where(is_last, 0.0, pltpu.roll(g, flat - 1, 1)).astype(bf16)
            gt[cols : 2 * cols, here] = g.astype(bf16)
            gt[2 * cols : 3 * cols, here] = jnp.where(is_first, 0.0, pltpu.roll(g, 1, 1)).astype(bf16)

    prepare(0)
    for i in range(STEPS):
        for h in range(i * step, (i + 1) * step):
            acopy[h].wait()
        if i + 1 < STEPS:
            prepare(i + 1)
        rhs = av[i * step : (i + 1) * step].reshape(step * flat, cin)
        term = jnp.dot(gt[:, (i * step + 1) * flat : ((i + 1) * step + 1) * flat], rhs, preferred_element_type=f32)
        acc[...] = term if i == 0 else acc[...] + term
    emit(acc, turned, outs, osem, me_ref[0], cols)


def next_kernel(shift, parts, me_ref, gt, av, *rest):
    outs = rest[:parts]
    acc, turned, osem = rest[parts:]
    height, batch, width, cin = av.shape
    flat = batch * width
    cols = gt.shape[0] // 3
    lhs = gt[:, (1 + shift) * flat : (1 + shift + height) * flat]
    acc[...] = jnp.dot(lhs, av[...].reshape(height * flat, cin), preferred_element_type=f32)
    emit(acc, turned, outs, osem, me_ref[0], cols)


def conv_first(a, g, me, parts):
    batch, height, width, cin = a.shape
    cols = g.shape[3]
    flat = batch * width
    res = pl.pallas_call(
        functools.partial(first_kernel, parts),
        out_shape=[jax.ShapeDtypeStruct((3, cin // parts, cols), f32)] * parts
        + [pltpu.VMEM((height, batch, width, cin), bf16), pltpu.VMEM((3 * cols, (height + 2) * flat), bf16)],
        in_specs=[SM, HB, HB],
        out_specs=[HB] * parts + [VM, VM],
        scratch_shapes=[
            pltpu.VMEM((batch, height, width, cols), bf16),
            pltpu.VMEM((3 * cols, cin), f32),
            pltpu.VMEM((3, cin, cols), f32),
            pltpu.SemaphoreType.DMA((height,)),
            pltpu.SemaphoreType.DMA((STEPS,)),
            pltpu.SemaphoreType.DMA((parts,)),
        ],
        compiler_params=pltpu.CompilerParams(vmem_limit_bytes=FIRST_VMEM),
        cost_estimate=pl.CostEstimate(flops=6 * cols * cin * height * flat, bytes_accessed=2 * (a.size + g.size), transcendentals=0),
        name="conv_first",
    )(me, g, a)
    return list(res[:parts]), res[parts], res[parts + 1]


def conv_next(av, gt, me, shift, parts):
    height, batch, width, cin = av.shape
    cols = gt.shape[0] // 3
    return list(pl.pallas_call(
        functools.partial(next_kernel, shift, parts),
        out_shape=[jax.ShapeDtypeStruct((3, cin // parts, cols), f32)] * parts,
        in_specs=[SM, VM, VM],
        out_specs=[HB] * parts,
        scratch_shapes=[pltpu.VMEM((3 * cols, cin), f32), pltpu.VMEM((3, cin, cols), f32), pltpu.SemaphoreType.DMA((parts,))],
        compiler_params=pltpu.CompilerParams(vmem_limit_bytes=NEXT_VMEM),
        cost_estimate=pl.CostEstimate(flops=6 * cols * cin * height * batch * width, bytes_accessed=12 * cin * cols, transcendentals=0),
        name="conv_next",
    )(me, gt, av))


def tile_terms(gt, rhs, lo, hi, flat, i):
    return jnp.dot(gt[:, (lo + 2 - i) * flat : (hi + 2 - i) * flat], rhs, preferred_element_type=f32)


def tile_columns(av, chip, tiles, lo, hi):
    _, batch, width, cin = av.shape
    lanes = cin // 4
    firsts = [pl.multiple_of(jnp.bitwise_xor(chip, q) * lanes, lanes) for q in tiles]
    return jnp.concatenate([av[lo:hi, :, :, pl.ds(f, lanes)].reshape((hi - lo) * batch * width, lanes) for f in firsts], axis=1)


def tile_store(value, i, taps, outs, me, cols):
    i = taps.index(i)
    is_lower = jnp.bitwise_and(me, 1) == 0
    depth = outs[0].shape[0] // (3 * len(taps))
    for q in range(len(outs) // 2):
        for j in range(3):
            turned = value[j * cols : (j + 1) * cols, q * 2 * depth : (q + 1) * 2 * depth].T
            lower, upper = turned[:depth], turned[depth:]
            here = slice((3 * i + j) * depth, (3 * i + j + 1) * depth)
            outs[2 * q][here, :] = jnp.where(is_lower, lower, upper)
            outs[2 * q + 1][here, :] = jnp.where(is_lower, upper, lower)


def near_kernel(bounds, taps, me_ref, g_hbm, a_hbm, *rest):
    outs = rest[:4]
    av, gt, gv, acc, asem, gsem = rest[4:]
    height, batch, width, _ = av.shape
    cols = gv.shape[3]
    flat = batch * width
    rows = 3 * cols
    me = me_ref[0]
    gends = [0] + [min(b + 1, height) for b in bounds[1:]]
    gcopy = [pltpu.make_async_copy(g_hbm.at[:, h], gv.at[:, h], gsem.at[h]) for h in range(height)]
    acopy = [pltpu.make_async_copy(a_hbm.at[:, h], av.at[h], asem.at[h]) for h in range(height)]
    order = gcopy[: gends[1]]
    for n in range(len(bounds) - 1):
        order += acopy[bounds[n] : bounds[n + 1]]
        if n + 2 < len(bounds):
            order += gcopy[gends[n + 1] : gends[n + 2]]
    for copy in order:
        copy.start()
    gt[:, 0:flat] = jnp.zeros((rows, flat), bf16)
    gt[:, (height + 1) * flat : (height + 2) * flat] = jnp.zeros((rows, flat), bf16)
    column = lax.broadcasted_iota(jnp.int32, (cols, flat), 1) % width
    is_last, is_first = column == width - 1, column == 0

    def prepare(lo, hi):
        for h in range(lo, hi):
            g = gv[:, h].reshape(flat, cols).T
            here = slice((h + 1) * flat, (h + 2) * flat)
            gt[0:cols, here] = jnp.where(is_last, jnp.zeros_like(g), pltpu.roll(g, flat - 1, 1))
            gt[cols : 2 * cols, here] = g
            gt[2 * cols : 3 * cols, here] = jnp.where(is_first, jnp.zeros_like(g), pltpu.roll(g, 1, 1))

    for h in range(gends[1]):
        gcopy[h].wait()

    @pl.when(me >= 0)
    def _():
        prepare(0, gends[1])

    for n in range(len(bounds) - 1):
        lo, hi = bounds[n], bounds[n + 1]
        for h in range(lo, hi):
            acopy[h].wait()
        if n + 2 < len(bounds):
            for h in range(gends[n + 1], gends[n + 2]):
                gcopy[h].wait()

        @pl.when(me >= 0)
        def _(n=n, lo=lo, hi=hi):
            is_end = n + 2 == len(bounds)
            if not is_end:
                prepare(gends[n + 1], gends[n + 2])
            rhs = tile_columns(av, me // 2, (1 + jnp.bitwise_and(me, 1), 2 - jnp.bitwise_and(me, 1)), lo, hi)
            for i in taps:
                here = slice(taps.index(i) * rows, (taps.index(i) + 1) * rows)
                term = tile_terms(gt, rhs, lo, hi, flat, i)
                if n > 0:
                    term = acc[here, :] + term
                if is_end:
                    tile_store(term, i, taps, outs, me, cols)
                else:
                    acc[here, :] = term


def held_kernel(near, taps, me_ref, gt, av, *outs):
    height, batch, width, _ = av.shape
    me = me_ref[0]
    core = jnp.bitwise_and(me, 1)
    rhs = tile_columns(av, me // 2, (1 + core, 2 - core) if near else (3, 0), 0, height)
    for i in taps:
        tile_store(tile_terms(gt, rhs, 0, height, batch * width, i), i, taps, outs, me, gt.shape[0] // 3)


def near_blocks(a, g, me, taps):
    batch, height, width, cin = a.shape
    cols = g.shape[3]
    lanes, flat = cin // 4, batch * width
    block = jax.ShapeDtypeStruct((3 * len(taps) * (lanes // 2), cols), f32)
    res = pl.pallas_call(
        functools.partial(near_kernel, [height * n // 32 for n in (0, 3, 8, 14, 20, 26, 32)], taps),
        out_shape=[block] * 4 + [pltpu.VMEM((height, batch, width, cin), bf16), pltpu.VMEM((3 * cols, (height + 2) * flat), bf16)],
        in_specs=[SM, HB, HB],
        out_specs=[VM] * 6,
        scratch_shapes=[
            pltpu.VMEM((batch, height, width, cols), bf16),
            pltpu.VMEM((3 * len(taps) * cols, 2 * lanes), f32),
            pltpu.SemaphoreType.DMA((height,)),
            pltpu.SemaphoreType.DMA((height,)),
        ],
        compiler_params=pltpu.CompilerParams(vmem_limit_bytes=NEAR_VMEM),
        cost_estimate=pl.CostEstimate(flops=12 * len(taps) * cols * lanes * height * flat, bytes_accessed=2 * (a.size + g.size), transcendentals=0),
        name="conv_near",
    )(me, g, a)
    return list(res[:4]), res[4], res[5]


def held_blocks(av, gt, me, near, taps):
    height, batch, width, cin = av.shape
    lanes = cin // 4
    cols = gt.shape[0] // 3
    block = jax.ShapeDtypeStruct((3 * len(taps) * (lanes // 2), cols), f32)
    return list(pl.pallas_call(
        functools.partial(held_kernel, near, taps),
        out_shape=[block] * 4,
        in_specs=[SM, VM, VM],
        out_specs=[VM] * 4,
        compiler_params=pltpu.CompilerParams(vmem_limit_bytes=NEXT_VMEM),
        cost_estimate=pl.CostEstimate(flops=12 * len(taps) * cols * lanes * height * batch * width, bytes_accessed=24 * len(taps) * lanes * cols, transcendentals=0),
        name="conv_near_rest" if near else "conv_far",
    )(me, gt, av))


def replica_of(me, flips, k):
    even, odd = flips[k]
    return jnp.bitwise_xor(me, even + jnp.bitwise_and(me, 1) * (odd - even))


def gram_kernel(jobs, pieces, flips, devices, me_ref, *rest):
    parts = len(pieces)
    count = 1 + max(n for piece in pieces for _, _, n in piece)
    arrays, before, (out, rowsums) = rest[:count], rest[count:-2], rest[-2:]
    me = me_ref[0]
    cols = arrays[0].shape[1]
    rowsums[...] = jnp.zeros_like(rowsums)
    size = rowsums.shape[0]
    number = lax.broadcasted_iota(jnp.int32, (size, 128), 0)
    at = jnp.full((size, 128), -1, jnp.int32)
    row = 0
    for lo, hi, pairs in jobs:
        for first in range(0, len(pairs), 16):
            some = pairs[first : first + 16]
            held = {}
            for k in sorted({n for pair in some for n in pair}):
                ((start, _, n),) = [p for p in pieces[k] if p[0] <= lo and hi <= p[1]]
                held[k] = (arrays[n], lo - start)

            def body(i, sums):
                x = {k: ref[pl.ds(pl.multiple_of(i * 8, 8) + skip, 8), :] for k, (ref, skip) in held.items()}
                return [s + x[k] * x[l] for s, (k, l) in zip(sums, some)]

            sums = lax.fori_loop(0, (hi - lo) // 8, body, [jnp.zeros((8, cols), f32) for _ in some], unroll=8)
            for s, (k, l) in zip(sums, some):
                rowsums[row : row + 1, :] = jnp.sum(s, axis=0, keepdims=True)
                a, b = replica_of(me, flips, k), replica_of(me, flips, l)
                at = jnp.where(number == row, jnp.minimum(a, b) * parts + jnp.maximum(a, b), at)
                row += 1
    place = lax.broadcasted_iota(jnp.int32, (size, 128), 1)
    values = jnp.sum(rowsums[...], axis=1, keepdims=True)
    for r in range(out.shape[-2]):
        total = jnp.sum(jnp.where(at == place + r * 128, values, 0.0), axis=0, keepdims=True)
        for part in before:
            total = total + part[r : r + 1, :]
        for n in range(max(devices, 1)):
            if devices:
                out[n, r : r + 1, :] = total
            else:
                out[r : r + 1, :] = total


def gram(jobs, pieces, arrays, before, me, flips, devices):
    parts = len(pieces)
    names = [{n for pair in pairs for n in pair} for _, _, pairs in jobs]
    used = sorted({n for k in range(parts) for lo, hi, n in pieces[k] for (jlo, jhi, _), ks in zip(jobs, names) if k in ks and lo <= jlo and jhi <= hi})
    near = [[(lo, hi, used.index(n)) for lo, hi, n in piece if n in used] for piece in pieces]
    rows = -(-parts * parts // 128)
    shape = (devices, rows, 128) if devices else (rows, 128)
    size = -(-sum(len(pairs) for _, _, pairs in jobs) // 8) * 8
    flat = [arrays[n] for n in used]
    return pl.pallas_call(
        functools.partial(gram_kernel, jobs, near, flips, devices),
        out_shape=jax.ShapeDtypeStruct(shape, f32),
        in_specs=[SM] + [VM] * (len(flat) + len(before)),
        out_specs=VM,
        scratch_shapes=[pltpu.VMEM((size, flat[0].shape[1]), f32)],
        compiler_params=pltpu.CompilerParams(vmem_limit_bytes=NEXT_VMEM),
        cost_estimate=pl.CostEstimate(flops=2 * 128 * sum((hi - lo) * len(pairs) for lo, hi, pairs in jobs), bytes_accessed=sum(4 * x.size for x in flat), transcendentals=0),
        name="gram",
    )(me, *flat, *before)


def mixes_of(sums, parts):
    rows = sums.shape[0]
    place = lax.broadcasted_iota(jnp.int32, (rows, 128), 0) * 128 + lax.broadcasted_iota(jnp.int32, (rows, 128), 1)
    g = {}
    for a in range(parts):
        for b in range(a, parts):
            g[a, b] = g[b, a] = jnp.sum(jnp.where(place == a * parts + b, sums, 0.0), axis=(0, 1), keepdims=True)
    factors = [None] * parts
    count, width = parts, 1
    while count > 1:
        coef = []
        for k in range(count // 2):
            p, qa, qb = g[2 * k, 2 * k + 1], g[2 * k, 2 * k] + 1e-6, g[2 * k + 1, 2 * k + 1] + 1e-6
            coef += [1.0 - p / (2.0 * qa), 1.0 - p / (2.0 * qb)]
        for r in range(parts):
            c = coef[r // width]
            factors[r] = c if factors[r] is None else factors[r] * c
        count, width = count // 2, width * 2
        new = {}
        for k in range(count):
            for l in range(k, count):
                new[k, l] = new[l, k] = sum(coef[x] * coef[y] * g[x, y] for x in (2 * k, 2 * k + 1) for y in (2 * l, 2 * l + 1))
        g = new
    return factors


def final_kernel(pieces, flips, me_ref, sums, weight, momentum, *rest):
    arrays, (weight_out, momentum_out, new_weight, new_momentum, sem) = rest[:-5], rest[-5:]
    parts = len(pieces)
    copies = []
    me = me_ref[0]
    factors = mixes_of(jnp.sum(sums[...], axis=0), parts)
    mine = []
    for k in range(parts):
        pick, replica = factors[0], replica_of(me, flips, k)
        for r in range(1, parts):
            pick = jnp.where(replica == r, factors[r], pick)
        mine.append(pick)
    step = weight.shape[0] // 9
    for first in range(0, weight.shape[0], step):
        here = slice(first, first + step)
        value = 0.9 * momentum[here, :]
        for k in range(parts):
            ((lo, n),) = [(lo, n) for lo, hi, n in pieces[k] if lo <= first < hi]
            value = value + mine[k] * arrays[n][first - lo : first - lo + step, :]
        new_momentum[here, :] = value
        new_weight[here, :] = weight[here, :] - 0.1 * value
        if (first // step) % 3 == 2:
            third = slice(first - 2 * step, first + step)
            for held, out in ((new_weight, weight_out), (new_momentum, momentum_out)):
                copies.append(pltpu.make_async_copy(held.at[third], out.at[third], sem.at[len(copies)]))
                copies[-1].start()
    for copy in copies:
        copy.wait()


def finish(sums, weight, momentum, pieces, arrays, me, flips):
    depth, cols = weight.shape[0], weight.shape[3]
    w, m = (jnp.transpose(x, (1, 2, 0, 3)).reshape(9 * depth, cols) for x in (weight, momentum))
    outs = pl.pallas_call(
        functools.partial(final_kernel, pieces, flips),
        out_shape=[jax.ShapeDtypeStruct(w.shape, f32)] * 2,
        in_specs=[SM] + [VM] * (3 + len(arrays)),
        out_specs=[HB, HB],
        scratch_shapes=[pltpu.VMEM(w.shape, f32), pltpu.VMEM(w.shape, f32), pltpu.SemaphoreType.DMA((6,))],
        compiler_params=pltpu.CompilerParams(vmem_limit_bytes=NEXT_VMEM),
        cost_estimate=pl.CostEstimate(flops=2 * w.size * len(pieces), bytes_accessed=4 * w.size * (len(pieces) + 4), transcendentals=0),
        name="final",
    )(me, sums, w, m, *arrays)
    return tuple(jnp.transpose(x.reshape(3, 3, depth, cols), (2, 0, 1, 3)) for x in outs)


def upper_pairs(parts):
    return [(k, l) for k in range(parts) for l in range(k, parts)]


def send(block, parts, flips):
    return lax.ppermute(block, "dp", [(r, r ^ flips[r % 2]) for r in range(parts)])


def by_rows(activations, out_grads, me, parts, devices):
    def exchange(blocks):
        blocks = [b.reshape(-1, b.shape[2]) for b in blocks]
        return blocks[:1] + [send(blocks[k], parts, (k, k)) for k in range(1, parts)]

    middle, av, gt = conv_first(activations, out_grads, me, parts)
    middle = exchange(middle)
    lower = exchange(conv_next(av, gt, me, 1, parts))
    upper = exchange(conv_next(av, gt, me, -1, parts))
    size = middle[0].shape[0]
    pieces = [[(i * size, (i + 1) * size, i * parts + k) for i in range(3)] for k in range(parts)]
    arrays, flips, partial = lower + middle + upper, [(k, k) for k in range(parts)], []
    for i in (1, 0, 2):
        job = (i * size, (i + 1) * size, upper_pairs(parts))
        partial = [gram([job], pieces, arrays, partial, me, flips, devices if i == 2 else 0)]
    return partial[0], pieces, arrays, flips


def by_chips(activations, out_grads, me, parts, devices):
    targets = [(2, 4), (3, 5), (4, 2), (5, 3)]

    def near_out(blocks):
        return [send(block, parts, t) for block, t in zip(blocks, targets)]

    def far_out(blocks):
        far = [send(blocks[k], parts, (6 + k, 6 + k)) for k in range(2)]
        return [blocks[2], send(blocks[3], parts, (1, 1))], far

    near, av, gt = near_blocks(activations, out_grads, me, (0, 1))
    near = near_out(near)
    far = held_blocks(av, gt, me, False, (0, 1))
    own, far = far_out(far)
    tail = held_blocks(av, gt, me, False, (2,))
    tail_own, tail = far_out(tail)
    rest = held_blocks(av, gt, me, True, (2,))
    rest = near_out(rest)
    flips = [(0, 0), (1, 1), (2, 4), (5, 3), (4, 2), (3, 5), (6, 6), (7, 7)]
    arrays = own + near + far + tail_own + rest + tail
    split = near[0].shape[0]
    whole = split + rest[0].shape[0]
    pieces = [[(0, split, k), (split, whole, parts + k)] for k in range(parts)]

    def pairs(low, high):
        return [pair for pair in upper_pairs(parts) if low <= pair[1] < high]

    sums = gram([(0, split, pairs(0, 6))], pieces, arrays, [], me, flips, 0)
    sums = gram([(0, split, pairs(6, 8))], pieces, arrays, [sums], me, flips, 0)
    late = [pair for pair in pairs(0, 8) if 4 in pair or 5 in pair]
    sums = gram([(split, whole, [pair for pair in pairs(0, 8) if pair not in late])], pieces, arrays, [sums], me, flips, 0)
    sums = gram([(split, whole, late)], pieces, arrays, [sums], me, flips, devices)
    return sums, pieces, arrays, flips


def shards(activations, out_grads, weight, momentum):
    parts = lax.axis_size("dp")
    devices = parts * lax.axis_size("chan")
    me = lax.axis_index("dp").reshape(1).astype(jnp.int32)
    four = parts == 8 and activations.shape[3] % 512 == 0
    sums, pieces, arrays, flips = (by_chips if four else by_rows)(activations, out_grads, me, parts, devices)
    sums = lax.all_to_all(sums, ("dp", "chan"), split_axis=0, concat_axis=0, tiled=True)
    return finish(sums, weight, momentum, pieces, arrays, me, flips)


FIRST_VMEM, NEXT_VMEM, NEAR_VMEM = 30 << 20, 30 << 20, 38 << 20


def solution(mesh):
    in_specs = (
        P("dp", None, None, None),
        P("dp", None, None, "chan"),
        P("dp", None, None, "chan"),
        P("dp", None, None, "chan"),
    )
    out_specs = (P("dp", None, None, "chan"), P("dp", None, None, "chan"))
    return jax.shard_map(shards, mesh=mesh, in_specs=in_specs, out_specs=out_specs, check_vma=False)
```
